32 devices in a mesh: dom: 8 (over z, y), wa: 4 (over x, core).
Axes of the slice: x: 2, y: 2, z: 4, core: 2. Of those that a mesh axis runs over, the one named last changes fastest.
Arguments:
- bond_feats: bfloat16 [2048, 256], P('dom'), may hold values from -6 to 6
- cotangent: bfloat16 [2048, 256], P('dom', 'wa'), may hold values from -6 to 6
- bond_count: int32 [8], P('dom'), may hold values from 128 to 256, as said below
- source: int32 [24576], P('dom'), may hold values from 0 to 319, as said below
- cosine: float32 [24576], P('dom'), may hold values from -1 to 1
- w_source: bfloat16 [256, 256], P(None, 'wa'), may hold values from -0.375 to 0.375
- w_target: bfloat16 [256, 256], P(None, 'wa'), may hold values from -0.375 to 0.375
- w_message: bfloat16 [256, 256], P(None, 'wa'), may hold values from -0.375 to 0.375
- w_self: bfloat16 [256, 256], P(None, 'wa'), may hold values from -0.375 to 0.375
- gate_angle: float32 [256], P('wa'), may hold values from -4 to 4
Outputs:
- bond_grad: bfloat16 [2048, 256], P('dom', 'wa')
- grad_source: float32 [256, 256], P('dom', 'wa')
- grad_target: float32 [256, 256], P('dom', 'wa')
- grad_message: float32 [256, 256], P('dom', 'wa')
- grad_self: float32 [256, 256], P('dom', 'wa')
- grad_gate: float32 [256], P('wa')
The draws below stay inside these ranges and needn't reach their ends.
Inputs may be any that keep to these rules, and one draw needn't show every extreme that they name: `bond_count`: every domain has 128 or more live bonds; some domain has all 256 live. `source`: each angle's other bond is a live row of the extended block of its domain: a ghost row (below 32 or at 288 or above) or 32 plus a live own row.
All inputs are finite; a program needn't handle non-finite values.
Results may differ from the reference program's by a relative error of at most 0.0085.
Values may be sent and summed in bfloat16 or wider, within the bound.
A program may use at most 64 MiB of HBM per device.

```python
import jax
import jax.numpy as jnp
from jax import lax

D = 256
BONDS_DOM = 256
ARITY = 12
GHOST = 32
BONDS = 2048
ANGLES = 24576


def shared_layout(key):
    domains = BONDS // BONDS_DOM
    counts = jax.random.randint(jax.random.fold_in(key, 11), (domains,), BONDS_DOM // 2, BONDS_DOM + 1)
    fullest = jax.random.randint(jax.random.fold_in(key, 12), (), 0, domains)
    counts = jnp.where(jnp.arange(domains, dtype=jnp.int32) == fullest, BONDS_DOM, counts).astype(jnp.int32)
    per_angle = jnp.broadcast_to(counts[:, None], (domains, ARITY * BONDS_DOM)).reshape(ANGLES)
    ghost_flag = jax.random.randint(jax.random.fold_in(key, 13), (ANGLES,), 0, 4) == 0
    ghost_pick = jax.random.randint(jax.random.fold_in(key, 14), (ANGLES,), 0, 2 * GHOST)
    ghost_index = jnp.where(ghost_pick < GHOST, ghost_pick, BONDS_DOM + ghost_pick)
    uniform_pick = jax.random.randint(jax.random.fold_in(key, 15), (ANGLES,), 0, per_angle)
    own_row = jnp.where(uniform_pick < per_angle - GHOST, uniform_pick, uniform_pick - (per_angle - GHOST) + BONDS_DOM - GHOST)
    sources = jnp.where(ghost_flag, ghost_index, GHOST + own_row).astype(jnp.int32)
    return (counts, sources)


def draw_bond_count(key, part):
    return shared_layout(key)[0]


def draw_source(key, part):
    return shared_layout(key)[1]


def level_of(own_key, dims, pieces, smallest, largest):
    level = 1.0
    for axis_at, shards_of in pieces:
        heights = jax.random.uniform(jax.random.fold_in(jax.random.fold_in(own_key, 6), axis_at), (shards_of,), jnp.float32, smallest / len(pieces), largest / len(pieces))
        level = level * jnp.repeat(jnp.exp(heights), dims[axis_at] // shards_of).reshape((-1,) + (1,) * (len(dims) - 1 - axis_at))
    return level


def normal_values(key, extent, scale, limit, shards=(), held_as=jnp.bfloat16):
    values = jax.random.normal(key, extent, jnp.float32) * scale
    if len(shards) > 0:
        values = level_of(key, extent, shards, -0.22, 0.18) * values
    return jnp.clip(values, min=-limit, max=limit).astype(held_as)


def setup_inputs(seed: int = 0) -> dict:
    key_list = jax.random.split(jax.random.key(seed), 11)
    return {
        "bond_feats": normal_values(key_list[0], (BONDS, D), 1.0, 6.0, ((0, 8),)),
        "cotangent": normal_values(key_list[1], (BONDS, D), 1.0, 6.0, ((0, 8), (1, 4))),
        "bond_count": draw_bond_count(jax.random.fold_in(key_list[10], 71), 0),
        "source": draw_source(jax.random.fold_in(key_list[10], 71), 0),
        "cosine": jnp.clip(jax.random.uniform(key_list[4], (ANGLES,), jnp.float32, -1.0, 1.0) * level_of(key_list[4], (ANGLES,), ((0, 8),), -0.4, 0.0), -1.0, 1.0),
        "w_source": normal_values(key_list[5], (D, D), D ** -0.5, 0.375, ((1, 4),)),
        "w_target": normal_values(key_list[6], (D, D), D ** -0.5, 0.375, ((1, 4),)),
        "w_message": normal_values(key_list[7], (D, D), D ** -0.5, 0.375, ((1, 4),)),
        "w_self": normal_values(key_list[8], (D, D), D ** -0.5, 0.375, ((1, 4),)),
        "gate_angle": normal_values(key_list[9], (D,), 1.0, 4.0, ((0, 4),), jnp.float32),
    }


epsilon = 1e-6


def silu_slope(values):
    sigma = jax.nn.sigmoid(values)
    return sigma * (1.0 + values * (1.0 - sigma))


def reference(bond_feats, cotangent, bond_count, source, cosine, w_source, w_target, w_message, w_self, gate_angle):
    domains = BONDS // BONDS_DOM
    width = bond_feats.shape[1]
    blocks = bond_feats.reshape(domains, BONDS_DOM, width)
    before = jnp.roll(blocks, 1, axis=0)[:, BONDS_DOM - GHOST:]
    after = jnp.roll(blocks, -1, axis=0)[:, :GHOST]
    extended_all = jnp.concatenate([before, blocks, after], axis=1)
    cot_blocks = cotangent.reshape(domains, BONDS_DOM, width)
    source_blocks = source.reshape(domains, ARITY * BONDS_DOM)
    cosine_blocks = cosine.reshape(domains, ARITY * BONDS_DOM)
    ext_rows = BONDS_DOM + 2 * GHOST

    def spread(values):
        return jnp.broadcast_to(values[:, None, :], (BONDS_DOM, ARITY, values.shape[1])).reshape(ARITY * BONDS_DOM, values.shape[1])

    def per_bond(values):
        return values.reshape(BONDS_DOM, ARITY, values.shape[1]).sum(axis=1)

    def domain_step(carry, inputs):
        extended, own_rows, cot_rows, count, sources, cosines = inputs
        rows = jnp.arange(BONDS_DOM, dtype=jnp.int32)
        live = ((rows < count - GHOST) | (rows >= BONDS_DOM - GHOST)).astype(jnp.float32)
        alive = jnp.broadcast_to(live[:, None], (BONDS_DOM, ARITY)).reshape(ARITY * BONDS_DOM)[:, None]
        proj_source = jnp.dot(extended, w_source, preferred_element_type=jnp.float32)
        proj_message = jnp.dot(extended, w_message, preferred_element_type=jnp.float32)
        proj_target = jnp.dot(own_rows, w_target, preferred_element_type=jnp.float32)
        base = jnp.dot(own_rows, w_self, preferred_element_type=jnp.float32)
        picked_source = jnp.take(proj_source, sources, axis=0)
        picked_message = jnp.take(proj_message, sources, axis=0)
        pre = picked_source + spread(proj_target) + cosines[:, None] * gate_angle[None, :]
        sigma = jax.nn.sigmoid(pre)
        gated = sigma * alive
        numer = per_bond(gated * picked_message)
        denom = per_bond(gated) + epsilon
        aggregate = numer / denom
        hidden = base + aggregate
        cot_live = cot_rows.astype(jnp.float32) * live[:, None]
        dhidden = cot_live * silu_slope(hidden)
        dnumer = dhidden / denom
        ddenom = -dhidden * aggregate / denom
        dgate = spread(dnumer) * picked_message + spread(ddenom)
        dmessage = gated * spread(dnumer)
        dpre = dgate * sigma * (1.0 - sigma) * alive
        dsource = jax.ops.segment_sum(dpre, sources, num_segments=ext_rows)
        dmsg_rows = jax.ops.segment_sum(dmessage, sources, num_segments=ext_rows)
        dtarget = per_bond(dpre)
        gate_term = jnp.sum(cosines[:, None] * dpre, axis=0)
        round_source = dsource.astype(jnp.bfloat16)
        round_message = dmsg_rows.astype(jnp.bfloat16)
        round_target = dtarget.astype(jnp.bfloat16)
        round_hidden = dhidden.astype(jnp.bfloat16)
        grad_one = jnp.dot(extended.T, round_source, preferred_element_type=jnp.float32)
        grad_two = jnp.dot(own_rows.T, round_target, preferred_element_type=jnp.float32)
        grad_four = jnp.dot(extended.T, round_message, preferred_element_type=jnp.float32)
        grad_five = jnp.dot(own_rows.T, round_hidden, preferred_element_type=jnp.float32)
        dext = jnp.dot(round_source, w_source.T, preferred_element_type=jnp.float32) + jnp.dot(round_message, w_message.T, preferred_element_type=jnp.float32)
        down = jnp.dot(round_target, w_target.T, preferred_element_type=jnp.float32) + jnp.dot(round_hidden, w_self.T, preferred_element_type=jnp.float32)
        new_carry = (carry[0] + grad_one, carry[1] + grad_two, carry[2] + grad_four, carry[3] + grad_five, carry[4] + gate_term)
        return new_carry, (dext, down + cot_live)

    zeros_square = jnp.zeros((width, width), jnp.float32)
    start = (zeros_square, zeros_square, zeros_square, zeros_square, jnp.zeros((width,), jnp.float32))
    totals, outputs = lax.scan(domain_step, start, (extended_all, blocks, cot_blocks, bond_count, source_blocks, cosine_blocks))
    dext_all, own_all = outputs
    own_total = own_all + dext_all[:, GHOST:GHOST + BONDS_DOM]
    from_next = jnp.roll(dext_all[:, :GHOST], -1, axis=0)
    from_prev = jnp.roll(dext_all[:, GHOST + BONDS_DOM:], 1, axis=0)
    own_total = own_total.at[:, BONDS_DOM - GHOST:].add(from_next)
    own_total = own_total.at[:, :GHOST].add(from_prev)
    bond_grad = own_total.reshape(BONDS, width).astype(jnp.bfloat16)
    return bond_grad, totals[0], totals[1], totals[2], totals[3], totals[4]
```

```python
import functools

import jax
import jax.numpy as jnp
from jax import lax
from jax.experimental import pallas as pl
from jax.experimental.pallas import tpu as pltpu
from jax.sharding import PartitionSpec as P

ARITY = 12
GHOST = 32
MESH = pl.DeviceIdType.MESH
LANES = 128

epsilon = 1e-06

NT = (((1,), (1,)), ((), ()))


def dot(a, b):
    return jnp.dot(a, b, preferred_element_type=jnp.float32)


def dot_nt(a, b):
    return lax.dot_general(a, b, NT, preferred_element_type=jnp.float32)


def split(values):
    high = values.astype(jnp.bfloat16)
    low = (values - high.astype(jnp.float32)).astype(jnp.bfloat16)
    return high, low


def flipped(values):
    return values.astype(jnp.float32).T


def kernel(
    n_dom,
    n_wa,
    fused,
    h_ref,
    cot_ref,
    count_ref,
    src_ref,
    cos_ref,
    ws_ref,
    wt_ref,
    wm_ref,
    wf_ref,
    ga_ref,
    bond_out,
    *refs,
):
    if fused:
        (g1_out, g2_out, g4_out, g5_out, gg_out) = refs[:5]
        refs = refs[5:]
    else:
        (g_out, gg_out) = refs[:2]
        refs = refs[2:]
    (
        wcat,
        wcat_t,
        h_t,
        gh,
        hot,
        table,
        picked,
        sig_s,
        dcol,
        own_w,
        wbuf,
        wrecv,
        gsend,
        grecv2,
        halo_send,
        halo_recv,
        wsend_sem,
        wrecv_sem,
        nsend_sem,
        nrecv_sem,
    ) = refs[:20]
    if fused:
        g_full, gbuf, grecv, gsend_sem, grecv_sem = refs[20:]
    dom = lax.axis_index("dom")
    wa = lax.axis_index("wa")
    capacity, depth = h_ref.shape
    cols = cot_ref.shape[1]
    up = (lax.rem(dom + 1, n_dom), wa)
    down = (lax.rem(dom + n_dom - 1, n_dom), wa)
    doms = range(1, n_dom) if fused else (1, n_dom - 1)

    barrier = pltpu.get_barrier_semaphore()
    for k in doms:
        pl.semaphore_signal(
            barrier, inc=1, device_id=(lax.rem(dom + k, n_dom), wa), device_id_type=MESH
        )
    for k in range(1, n_wa):
        pl.semaphore_signal(
            barrier, inc=1, device_id=(dom, lax.rem(wa + k, n_wa)), device_id_type=MESH
        )
    weights = jnp.concatenate([ws_ref[...], wm_ref[...], wt_ref[...], wf_ref[...]], axis=1)
    wcat[...] = weights
    wcat_t[...] = flipped(weights).astype(jnp.bfloat16)
    pl.semaphore_wait(barrier, len(doms) + n_wa - 1)

    to_up = pltpu.make_async_remote_copy(
        src_ref=h_ref.at[pl.ds(capacity - GHOST, GHOST), :],
        dst_ref=gh.at[pl.ds(0, GHOST), :],
        send_sem=halo_send.at[0],
        recv_sem=halo_recv.at[0],
        device_id=up,
        device_id_type=MESH,
    )
    to_down = pltpu.make_async_remote_copy(
        src_ref=h_ref.at[pl.ds(0, GHOST), :],
        dst_ref=gh.at[pl.ds(GHOST, GHOST), :],
        send_sem=halo_send.at[1],
        recv_sem=halo_recv.at[1],
        device_id=down,
        device_id_type=MESH,
    )
    to_up.start()
    to_down.start()

    ext = capacity + 2 * GHOST
    row_id = lax.broadcasted_iota(jnp.int32, (ext, capacity), 0)
    for j in range(ARITY):
        s = src_ref[j : j + 1, :]
        s = jnp.where(
            s < GHOST, s + capacity, jnp.where(s < capacity + GHOST, s - GHOST, s)
        )
        hot[:, j * capacity : (j + 1) * capacity] = jnp.where(
            row_id == s, 1.0, 0.0
        ).astype(jnp.bfloat16)
    h_t[:, :capacity] = flipped(h_ref[...]).astype(jnp.bfloat16)
    proj = dot_nt(wcat_t[...], h_ref[...])
    lane = lax.broadcasted_iota(jnp.int32, (1, capacity), 1)
    count = count_ref[0]
    live = jnp.where(
        (lane < count - GHOST) | (lane >= capacity - GHOST), 1.0, 0.0
    ).astype(jnp.float32)
    cot_live = flipped(cot_ref[...]) * live
    angle = jnp.broadcast_to(ga_ref[...], (LANES, cols)).T
    high, low = split(proj[: 2 * cols])
    table[: 2 * cols, :capacity] = high
    table[2 * cols :, :capacity] = low

    to_up.wait()
    to_down.wait()
    proj_g = dot_nt(wcat_t[: 2 * cols, :], gh[...])
    high, low = split(proj_g)
    table[: 2 * cols, capacity:] = high
    table[2 * cols :, capacity:] = low
    h_t[:, capacity:] = flipped(gh[...]).astype(jnp.bfloat16)

    picked[...] = dot(table[...], hot[...])

    parts_z = []
    parts_t = []
    gate_sum = jnp.zeros((cols, LANES), jnp.float32)
    for half in range(capacity // LANES):
        at = half * LANES
        q2 = proj[2 * cols : 3 * cols, at : at + LANES]
        base = proj[3 * cols :, at : at + LANES]
        lv = live[:, at : at + LANES]
        numer = jnp.zeros((cols, LANES), jnp.float32)
        denom = jnp.zeros((cols, LANES), jnp.float32)
        for j in range(ARITY):
            here = pl.ds(j * capacity + at, LANES)
            p1 = picked[0:cols, here] + picked[2 * cols : 3 * cols, here]
            p4 = picked[cols : 2 * cols, here] + picked[3 * cols :, here]
            pre = p1 + q2 + cos_ref[j : j + 1, at : at + LANES] * angle
            sig = jax.nn.sigmoid(pre)
            sig_s[:, here] = sig
            picked[cols : 2 * cols, here] = p4
            numer = numer + sig * p4
            denom = denom + sig
        inverse = 1.0 / (denom * lv + epsilon)
        agg = numer * lv * inverse
        z = base + agg
        sz = jax.nn.sigmoid(z)
        dz = cot_live[:, at : at + LANES] * (sz * (1.0 + z * (1.0 - sz)))
        dnum = dz * inverse
        dq2 = jnp.zeros((cols, LANES), jnp.float32)
        for j in range(ARITY):
            here = pl.ds(j * capacity + at, LANES)
            sig = sig_s[:, here]
            dmsg = sig * dnum
            dpre = dmsg * (picked[cols : 2 * cols, here] - agg) * (1.0 - sig)
            dq2 = dq2 + dpre
            gate_sum = gate_sum + cos_ref[j : j + 1, at : at + LANES] * dpre
            dcol[:cols, here] = dpre.astype(jnp.bfloat16)
            dcol[cols:, here] = dmsg.astype(jnp.bfloat16)
        parts_z.append(dz.astype(jnp.bfloat16))
        parts_t.append(dq2.astype(jnp.bfloat16))

    rows = dot_nt(dcol[...], hot[...]).astype(jnp.bfloat16)
    dcat = jnp.concatenate(
        [
            rows[:, :capacity],
            jnp.concatenate(parts_t, axis=1),
            jnp.concatenate(parts_z, axis=1),
        ],
        axis=0,
    )
    dghost = rows[:, capacity:]

    whole = dot(wcat[...], dcat)
    whole_g = dot(wcat[:, : 2 * cols], dghost)
    whole_g = jnp.concatenate(
        [whole_g, jnp.zeros((depth, LANES - 2 * GHOST), jnp.float32)], axis=1
    )
    own_w[:, :capacity] = whole
    own_w[:, capacity:] = whole_g
    for c in range(n_wa):
        wbuf[c, :, :capacity] = whole[c * cols : (c + 1) * cols].astype(jnp.bfloat16)
        wbuf[c, :, capacity:] = whole_g[c * cols : (c + 1) * cols].astype(jnp.bfloat16)
    wcopies = []
    for k in range(1, n_wa):
        to = lax.rem(wa + k, n_wa)
        copy = pltpu.make_async_remote_copy(
            src_ref=wbuf.at[to],
            dst_ref=wrecv.at[k - 1],
            send_sem=wsend_sem.at[k - 1],
            recv_sem=wrecv_sem.at[k - 1],
            device_id=(dom, to),
            device_id_type=MESH,
        )
        copy.start()
        wcopies.append(copy)

    grads = dot_nt(h_t[:, :capacity], dcat)
    grads_g = dot_nt(h_t[:, capacity:], dghost)
    grads = jnp.concatenate([grads[:, : 2 * cols] + grads_g, grads[:, 2 * cols :]], axis=1)
    high, low = split(gate_sum)
    ones = jnp.ones((16, LANES), jnp.bfloat16)
    gate_row = dot_nt(ones, high) + dot_nt(ones, low)
    gcopies = []
    if fused:
        chunk = depth // n_dom
        g_full[...] = grads
        row16 = lax.broadcasted_iota(jnp.int32, (16, cols), 0)
        ghigh = gate_row.astype(jnp.bfloat16).astype(jnp.float32)
        gate_block = jnp.where(row16 == 0, ghigh, gate_row - ghigh)
        gate_block = jnp.concatenate(
            [gate_block, jnp.zeros((16, 4 * cols - cols), jnp.float32)], axis=1
        ).astype(jnp.bfloat16)
        for i in range(n_dom):
            gbuf[i, :chunk, :] = grads[i * chunk : (i + 1) * chunk].astype(jnp.bfloat16)
            gbuf[i, chunk:, :] = gate_block
        for k in range(1, n_dom):
            to = lax.rem(dom + k, n_dom)
            copy = pltpu.make_async_remote_copy(
                src_ref=gbuf.at[to],
                dst_ref=grecv.at[k - 1],
                send_sem=gsend_sem.at[k - 1],
                recv_sem=grecv_sem.at[k - 1],
                device_id=(to, wa),
                device_id_type=MESH,
            )
            copy.start()
            gcopies.append(copy)
    else:
        g_out[...] = grads
        gg_out[...] = gate_row[0:1]

    for copy in wcopies:
        copy.wait()
    mine = pl.ds(pl.multiple_of(wa * cols, cols), cols)
    total = own_w[mine, :]
    for k in range(n_wa - 1):
        total = total + wrecv[k].astype(jnp.float32)
    gsend[...] = total[:, capacity:]
    ncopies = []
    for i, to in enumerate((up, down)):
        copy = pltpu.make_async_remote_copy(
            src_ref=gsend,
            dst_ref=grecv2.at[i],
            send_sem=nsend_sem.at[i],
            recv_sem=nrecv_sem.at[i],
            device_id=to,
            device_id_type=MESH,
        )
        copy.start()
        ncopies.append(copy)

    own = total[:, :capacity] + cot_live
    if fused:
        for copy in gcopies:
            copy.wait()
        acc = g_full[pl.ds(pl.multiple_of(dom * chunk, chunk), chunk), :]
        gate = gate_row[0:1]
        for k in range(n_dom - 1):
            acc = acc + grecv[k, :chunk, :].astype(jnp.float32)
            pair = grecv[k, chunk:, :cols].astype(jnp.float32)
            gate = gate + pair[0:1] + pair[1:2]
        g1_out[...] = acc[:, :cols]
        g4_out[...] = acc[:, cols : 2 * cols]
        g2_out[...] = acc[:, 2 * cols : 3 * cols]
        g5_out[...] = acc[:, 3 * cols :]
        gg_out[...] = gate

    for copy in ncopies:
        copy.wait()
    lane_t = lax.broadcasted_iota(jnp.int32, (cols, LANES), 1)
    below = pltpu.roll(grecv2[0], LANES - GHOST, 1)
    above = pltpu.roll(grecv2[1], LANES - GHOST, 1)
    first = own[:, :LANES] + jnp.where(lane_t < GHOST, below, 0.0)
    last = own[:, capacity - LANES :] + jnp.where(lane_t >= LANES - GHOST, above, 0.0)
    result = jnp.concatenate([first, own[:, LANES : capacity - LANES], last], axis=1) if capacity > 2 * LANES else jnp.concatenate([first, last], axis=1)
    bond_out[...] = result.T.astype(jnp.bfloat16)


def per_device(
    n_dom,
    n_wa,
    bond_feats,
    cotangent,
    bond_count,
    source,
    cosine,
    w_source,
    w_target,
    w_message,
    w_self,
    gate_angle,
):
    capacity, depth = bond_feats.shape
    cols = cotangent.shape[1]
    angles = source.shape[0]
    ext = capacity + 2 * GHOST
    chunk = depth // n_dom
    fused = chunk % 16 == 0
    src = source.reshape(capacity, ARITY).T
    cos = cosine.reshape(capacity, ARITY).T
    f32, bf16 = jnp.float32, jnp.bfloat16
    vmem = pl.BlockSpec(memory_space=pltpu.VMEM)
    outs = [jax.ShapeDtypeStruct((capacity, cols), bf16)]
    if fused:
        outs += [jax.ShapeDtypeStruct((chunk, cols), f32)] * 4
    else:
        outs += [jax.ShapeDtypeStruct((depth, 4 * cols), f32)]
    outs += [jax.ShapeDtypeStruct((1, cols), f32)]
    dma = pltpu.SemaphoreType.DMA
    scratch = [
        pltpu.VMEM((depth, 4 * cols), bf16),
        pltpu.VMEM((4 * cols, depth), bf16),
        pltpu.VMEM((depth, ext), bf16),
        pltpu.VMEM((2 * GHOST, depth), bf16),
        pltpu.VMEM((ext, angles), bf16),
        pltpu.VMEM((4 * cols, ext), bf16),
        pltpu.VMEM((4 * cols, angles), f32),
        pltpu.VMEM((cols, angles), f32),
        pltpu.VMEM((2 * cols, angles), bf16),
        pltpu.VMEM((depth, capacity + LANES), f32),
        pltpu.VMEM((n_wa, cols, capacity + LANES), bf16),
        pltpu.VMEM((n_wa - 1, cols, capacity + LANES), bf16),
        pltpu.VMEM((cols, LANES), f32),
        pltpu.VMEM((2, cols, LANES), f32),
        dma((2,)),
        dma((2,)),
        dma((n_wa - 1,)),
        dma((n_wa - 1,)),
        dma((2,)),
        dma((2,)),
    ]
    if fused:
        scratch += [
            pltpu.VMEM((depth, 4 * cols), f32),
            pltpu.VMEM((n_dom, chunk + 16, 4 * cols), bf16),
            pltpu.VMEM((n_dom - 1, chunk + 16, 4 * cols), bf16),
            dma((n_dom - 1,)),
            dma((n_dom - 1,)),
        ]
    results = pl.pallas_call(
        functools.partial(kernel, n_dom, n_wa, fused),
        out_shape=outs,
        in_specs=[vmem, vmem, pl.BlockSpec(memory_space=pltpu.SMEM)] + [vmem] * 7,
        out_specs=[vmem] * len(outs),
        scratch_shapes=scratch,
        compiler_params=pltpu.CompilerParams(
            collective_id=0, has_side_effects=True, vmem_limit_bytes=48 << 20
        ),
        name="line_graph_backward",
    )(
        bond_feats,
        cotangent,
        bond_count,
        src,
        cos,
        w_source,
        w_target,
        w_message,
        w_self,
        gate_angle.reshape(1, cols),
    )
    if fused:
        bond_grad, one, two, four, five, gate = results
        return bond_grad, one, two, four, five, gate.reshape(cols)
    bond_grad, grads, gate = results
    mine = lax.psum_scatter(grads, "dom", scatter_dimension=0, tiled=True)
    gate = lax.psum(gate.reshape(cols), "dom")
    one, four, two, five = (mine[:, i * cols : (i + 1) * cols] for i in range(4))
    return bond_grad, one, two, four, five, gate


def solution(mesh):
    return jax.shard_map(
        functools.partial(per_device, mesh.shape["dom"], mesh.shape["wa"]),
        mesh=mesh,
        in_specs=(
            P("dom", None),
            P("dom", "wa"),
            P("dom"),
            P("dom"),
            P("dom"),
            P(None, "wa"),
            P(None, "wa"),
            P(None, "wa"),
            P(None, "wa"),
            P("wa"),
        ),
        out_specs=(
            P("dom", "wa"),
            P("dom", "wa"),
            P("dom", "wa"),
            P("dom", "wa"),
            P("dom", "wa"),
            P("wa"),
        ),
        check_vma=False,
    )
```

```python
import functools

import jax
import jax.numpy as jnp
from jax import lax
from jax.experimental import pallas as pl
from jax.experimental.pallas import tpu as pltpu
from jax.sharding import PartitionSpec as P

ARITY = 12
GHOST = 32
MESH = pl.DeviceIdType.MESH
LANES = 128

epsilon = 1e-06

NT = (((1,), (1,)), ((), ()))


def dot(a, b):
    return jnp.dot(a, b, preferred_element_type=jnp.float32)


def dot_nt(a, b):
    return lax.dot_general(a, b, NT, preferred_element_type=jnp.float32)


def split(values):
    high = values.astype(jnp.bfloat16)
    low = (values - high.astype(jnp.float32)).astype(jnp.bfloat16)
    return high, low


def flipped(values):
    return values.astype(jnp.float32).T


def slot_major(src, cos, capacity):
    rows = src.shape[0]
    c_hi = cos.astype(jnp.bfloat16).astype(jnp.float32)
    parts = [(src >> 4).astype(jnp.float32), (src & 15).astype(jnp.float32), c_hi, cos - c_hi]
    a = lax.broadcasted_iota(jnp.int32, (LANES, 4 * LANES), 0)
    z = lax.broadcasted_iota(jnp.int32, (LANES, 4 * LANES), 1)
    turn = (8 * ARITY) * (z // LANES)
    mirror = jnp.where(a == (LANES - 1 + turn - z) % LANES, 1.0, 0.0).astype(jnp.bfloat16)
    mixed = dot(jnp.concatenate(parts, axis=0).astype(jnp.bfloat16), mirror)
    packed = jnp.concatenate(
        [
            jnp.concatenate(
                [mixed[i * rows : (i + 1) * rows, m * LANES : (m + 1) * LANES] for m in range(4)], axis=0
            )
            for i in range(4)
        ],
        axis=1,
    ).astype(jnp.bfloat16)
    b = lax.broadcasted_iota(jnp.int32, (capacity, 4 * rows), 0)
    q = lax.broadcasted_iota(jnp.int32, (capacity, 4 * rows), 1)
    want = ((b // 8) % 4) * rows + (ARITY * b) // LANES
    x0 = dot(jnp.where(q == want, 1.0, 0.0).astype(jnp.bfloat16), packed)
    x1 = dot(jnp.where(q == want + 1, 1.0, 0.0).astype(jnp.bfloat16), packed)
    bb = lax.broadcasted_iota(jnp.int32, (capacity, LANES), 0)
    p = lax.broadcasted_iota(jnp.int32, (capacity, LANES), 1)
    at = (LANES - 1 + 8 * ARITY * ((bb // 8) % 4) - p) % LANES
    first = at >= (ARITY * bb) % LANES
    def finish(v0, v1):
        v = jnp.where(first, v0, v1).reshape(capacity // 8, 8, LANES)
        v = pltpu.roll(v, 0, 2, stride=ARITY, stride_axis=1).reshape(capacity, LANES)
        return v.T[LANES - 16 :]
    s = finish(x0[:, :LANES] * 16.0 + x0[:, LANES:2*LANES], x1[:, :LANES] * 16.0 + x1[:, LANES:2*LANES])
    c = finish(x0[:, 2*LANES:3*LANES] + x0[:, 3*LANES:], x1[:, 2*LANES:3*LANES] + x1[:, 3*LANES:])
    return s, c


def kernel(
    n_dom,
    n_wa,
    fused,
    h_hbm,
    cot_hbm,
    count_hbm,
    src_hbm,
    cos_hbm,
    ws_hbm,
    wt_hbm,
    wm_hbm,
    wf_hbm,
    ga_hbm,
    bond_out,
    *refs,
):
    if fused:
        (g1_out, g2_out, g4_out, g5_out, gg_out) = refs[:5]
        refs = refs[5:]
    else:
        (g_out, gg_out) = refs[:2]
        refs = refs[2:]
    (
        wcat,
        wcat_t,
        h_t,
        gh,
        hot,
        table,
        picked,
        sig_s,
        dcol,
        own_w,
        wbuf,
        wrecv,
        gsend,
        grecv2,
        halo_send,
        halo_recv,
        wsend_sem,
        wrecv_sem,
        nsend_sem,
        nrecv_sem,
        h_ref,
        cot_ref,
        count_ref,
        src_ref,
        cosine_ref,
        ga_ref,
        cos_ref,
        in_sem,
    ) = refs[:28]
    if fused:
        g_full, gbuf, grecv, gsend_sem, grecv_sem = refs[28:]
    dom = lax.axis_index("dom")
    wa = lax.axis_index("wa")
    capacity, depth = h_ref.shape
    cols = cot_ref.shape[0]
    up = (lax.rem(dom + 1, n_dom), wa)
    down = (lax.rem(dom + n_dom - 1, n_dom), wa)
    doms = range(1, n_dom) if fused else (1, n_dom - 1)

    barrier = pltpu.get_barrier_semaphore()
    for k in doms:
        pl.semaphore_signal(
            barrier, inc=1, device_id=(lax.rem(dom + k, n_dom), wa), device_id_type=MESH
        )
    for k in range(1, n_wa):
        pl.semaphore_signal(
            barrier, inc=1, device_id=(dom, lax.rem(wa + k, n_wa)), device_id_type=MESH
        )
    loads = []
    pairs = [
        (src_hbm, src_ref),
        (cos_hbm, cosine_ref),
        (h_hbm, h_ref),
        (count_hbm, count_ref),
        (cot_hbm, cot_ref),
        (ga_hbm, ga_ref),
    ]
    for i, w in enumerate((ws_hbm, wm_hbm, wt_hbm, wf_hbm)):
        pairs.append((w, wcat_t.at[pl.ds(i * cols, cols), :]))
    for i, (ours, to) in enumerate(pairs):
        copy = pltpu.make_async_copy(ours, to, in_sem.at[i])
        copy.start()
        loads.append(copy)
    loads[0].wait()
    loads[1].wait()
    sources, cosines = slot_major(src_ref[...], cosine_ref[...], capacity)
    cos_ref[...] = cosines
    pl.semaphore_wait(barrier, len(doms) + n_wa - 1)

    to_up = pltpu.make_async_remote_copy(
        src_ref=h_hbm.at[pl.ds(capacity - GHOST, GHOST), :],
        dst_ref=gh.at[pl.ds(0, GHOST), :],
        send_sem=halo_send.at[0],
        recv_sem=halo_recv.at[0],
        device_id=up,
        device_id_type=MESH,
    )
    to_down = pltpu.make_async_remote_copy(
        src_ref=h_hbm.at[pl.ds(0, GHOST), :],
        dst_ref=gh.at[pl.ds(GHOST, GHOST), :],
        send_sem=halo_send.at[1],
        recv_sem=halo_recv.at[1],
        device_id=down,
        device_id_type=MESH,
    )
    to_up.start()
    to_down.start()

    ext = capacity + 2 * GHOST
    row_id = (
        lax.broadcasted_iota(jnp.int32, (capacity, capacity), 0)
        .astype(jnp.float32)
        .astype(jnp.bfloat16)
    )
    one = jnp.ones((), jnp.bfloat16)
    zero = jnp.zeros((), jnp.bfloat16)
    for j in range(ARITY):
        s = sources[15 - j : 16 - j, :]
        after = s >= capacity + GHOST
        own_row = jnp.where((s < GHOST) | after, 512.0, s - GHOST)
        side = jnp.where(s < GHOST, s, jnp.where(after, s - capacity, 512.0))
        here = pl.ds(j * capacity, capacity)
        hot[:capacity, here] = jnp.where(row_id == own_row.astype(jnp.bfloat16), one, zero)
        hot[capacity:, here] = jnp.where(
            row_id[: 2 * GHOST] == side.astype(jnp.bfloat16), one, zero
        )
    for copy in loads[2:]:
        copy.wait()
    h_t[:, :capacity] = flipped(h_ref[...]).astype(jnp.bfloat16)
    wcat[...] = flipped(wcat_t[...]).astype(jnp.bfloat16)
    proj = dot_nt(wcat_t[...], h_ref[...])
    lane = lax.broadcasted_iota(jnp.int32, (1, capacity), 1)
    count = count_ref[0]
    live = jnp.where(
        (lane < count - GHOST) | (lane >= capacity - GHOST), 1.0, 0.0
    ).astype(jnp.float32)
    cot_live = cot_ref[...].astype(jnp.float32) * live
    angle = jnp.broadcast_to(ga_ref[...], (LANES, cols)).T
    high, low = split(proj[: 2 * cols])
    table[: 2 * cols, :capacity] = high
    table[2 * cols :, :capacity] = low

    to_up.wait()
    to_down.wait()
    proj_g = dot_nt(wcat_t[: 2 * cols, :], gh[...])
    high, low = split(proj_g)
    table[: 2 * cols, capacity:] = high
    table[2 * cols :, capacity:] = low
    h_t[:, capacity:] = flipped(gh[...]).astype(jnp.bfloat16)

    picked[...] = dot(table[...], hot[...])

    parts_z = []
    parts_t = []
    gate_sum = jnp.zeros((cols, LANES), jnp.float32)
    for half in range(capacity // LANES):
        at = half * LANES
        q2 = proj[2 * cols : 3 * cols, at : at + LANES]
        base = proj[3 * cols :, at : at + LANES]
        lv = live[:, at : at + LANES]
        numer = jnp.zeros((cols, LANES), jnp.float32)
        denom = jnp.zeros((cols, LANES), jnp.float32)
        for j in range(ARITY):
            here = pl.ds(j * capacity + at, LANES)
            p1 = picked[0:cols, here] + picked[2 * cols : 3 * cols, here]
            p4 = picked[cols : 2 * cols, here] + picked[3 * cols :, here]
            pre = p1 + q2 + cos_ref[15 - j : 16 - j, at : at + LANES] * angle
            sig = jax.nn.sigmoid(pre)
            sig_s[:, here] = sig
            picked[cols : 2 * cols, here] = p4
            numer = numer + sig * p4
            denom = denom + sig
        inverse = 1.0 / (denom * lv + epsilon)
        agg = numer * lv * inverse
        z = base + agg
        sz = jax.nn.sigmoid(z)
        dz = cot_live[:, at : at + LANES] * (sz * (1.0 + z * (1.0 - sz)))
        dnum = dz * inverse
        dq2 = jnp.zeros((cols, LANES), jnp.float32)
        for j in range(ARITY):
            here = pl.ds(j * capacity + at, LANES)
            sig = sig_s[:, here]
            dmsg = sig * dnum
            dpre = dmsg * (picked[cols : 2 * cols, here] - agg) * (1.0 - sig)
            dq2 = dq2 + dpre
            gate_sum = gate_sum + cos_ref[15 - j : 16 - j, at : at + LANES] * dpre
            dcol[:cols, here] = dpre.astype(jnp.bfloat16)
            dcol[cols:, here] = dmsg.astype(jnp.bfloat16)
        parts_z.append(dz.astype(jnp.bfloat16))
        parts_t.append(dq2.astype(jnp.bfloat16))

    rows = dot_nt(dcol[...], hot[...]).astype(jnp.bfloat16)
    dcat = jnp.concatenate(
        [
            rows[:, :capacity],
            jnp.concatenate(parts_t, axis=1),
            jnp.concatenate(parts_z, axis=1),
        ],
        axis=0,
    )
    dghost = rows[:, capacity:]

    whole = dot(wcat[...], dcat)
    whole_g = dot(wcat[:, : 2 * cols], dghost)
    whole_g = jnp.concatenate(
        [whole_g, jnp.zeros((depth, LANES - 2 * GHOST), jnp.float32)], axis=1
    )
    own_w[:, :capacity] = whole
    own_w[:, capacity:] = whole_g
    for c in range(n_wa):
        wbuf[c, :, :capacity] = whole[c * cols : (c + 1) * cols].astype(jnp.bfloat16)
        wbuf[c, :, capacity:] = whole_g[c * cols : (c + 1) * cols].astype(jnp.bfloat16)
    wcopies = []
    for k in range(1, n_wa):
        to = lax.rem(wa + k, n_wa)
        copy = pltpu.make_async_remote_copy(
            src_ref=wbuf.at[to],
            dst_ref=wrecv.at[k - 1],
            send_sem=wsend_sem.at[k - 1],
            recv_sem=wrecv_sem.at[k - 1],
            device_id=(dom, to),
            device_id_type=MESH,
        )
        copy.start()
        wcopies.append(copy)

    grads = dot_nt(h_t[:, :capacity], dcat)
    grads_g = dot_nt(h_t[:, capacity:], dghost)
    grads = jnp.concatenate([grads[:, : 2 * cols] + grads_g, grads[:, 2 * cols :]], axis=1)
    high, low = split(gate_sum)
    ones = jnp.ones((16, LANES), jnp.bfloat16)
    gate_row = dot_nt(ones, high) + dot_nt(ones, low)
    gcopies = []
    if fused:
        chunk = depth // n_dom
        g_full[...] = grads
        row16 = lax.broadcasted_iota(jnp.int32, (16, cols), 0)
        ghigh = gate_row.astype(jnp.bfloat16).astype(jnp.float32)
        gate_block = jnp.where(row16 == 0, ghigh, gate_row - ghigh)
        gate_block = jnp.concatenate(
            [gate_block, jnp.zeros((16, 4 * cols - cols), jnp.float32)], axis=1
        ).astype(jnp.bfloat16)
        for i in range(n_dom):
            gbuf[i, :chunk, :] = grads[i * chunk : (i + 1) * chunk].astype(jnp.bfloat16)
            gbuf[i, chunk:, :] = gate_block
        for k in range(1, n_dom):
            to = lax.rem(dom + k, n_dom)
            copy = pltpu.make_async_remote_copy(
                src_ref=gbuf.at[to],
                dst_ref=grecv.at[k - 1],
                send_sem=gsend_sem.at[k - 1],
                recv_sem=grecv_sem.at[k - 1],
                device_id=(to, wa),
                device_id_type=MESH,
            )
            copy.start()
            gcopies.append(copy)
    else:
        g_out[...] = grads
        gg_out[...] = gate_row[0:1]

    for copy in wcopies:
        copy.wait()
    mine = pl.ds(pl.multiple_of(wa * cols, cols), cols)
    total = own_w[mine, :]
    for k in range(n_wa - 1):
        total = total + wrecv[k].astype(jnp.float32)
    gsend[...] = total[:, capacity:].astype(jnp.bfloat16)
    ncopies = []
    for i, to in enumerate((up, down)):
        copy = pltpu.make_async_remote_copy(
            src_ref=gsend,
            dst_ref=grecv2.at[i],
            send_sem=nsend_sem.at[i],
            recv_sem=nrecv_sem.at[i],
            device_id=to,
            device_id_type=MESH,
        )
        copy.start()
        ncopies.append(copy)

    own = total[:, :capacity] + cot_live
    if fused:
        for copy in gcopies:
            copy.wait()
        acc = g_full[pl.ds(pl.multiple_of(dom * chunk, chunk), chunk), :]
        gate = gate_row[0:1]
        for k in range(n_dom - 1):
            acc = acc + grecv[k, :chunk, :].astype(jnp.float32)
            pair = grecv[k, chunk:, :cols].astype(jnp.float32)
            gate = gate + pair[0:1] + pair[1:2]
        g1_out[...] = acc[:, :cols]
        g4_out[...] = acc[:, cols : 2 * cols]
        g2_out[...] = acc[:, 2 * cols : 3 * cols]
        g5_out[...] = acc[:, 3 * cols :]
        gg_out[...] = gate

    for copy in ncopies:
        copy.wait()
    lane_t = lax.broadcasted_iota(jnp.int32, (cols, LANES), 1)
    below = pltpu.roll(grecv2[0].astype(jnp.float32), LANES - GHOST, 1)
    above = pltpu.roll(grecv2[1].astype(jnp.float32), LANES - GHOST, 1)
    first = own[:, :LANES] + jnp.where(lane_t < GHOST, below, 0.0)
    last = own[:, capacity - LANES :] + jnp.where(lane_t >= LANES - GHOST, above, 0.0)
    result = jnp.concatenate([first, own[:, LANES : capacity - LANES], last], axis=1) if capacity > 2 * LANES else jnp.concatenate([first, last], axis=1)
    bond_out[...] = result.astype(jnp.bfloat16)


def put_out(*refs):
    count = len(refs) // 2
    sem = refs[-1]
    copies = [
        pltpu.make_async_copy(refs[i], refs[count + i], sem.at[i]) for i in range(count)
    ]
    for copy in copies:
        copy.start()
    for copy in copies:
        copy.wait()


def per_device(
    n_dom,
    n_wa,
    bond_feats,
    cotangent,
    bond_count,
    source,
    cosine,
    w_source,
    w_target,
    w_message,
    w_self,
    gate_angle,
):
    capacity, depth = bond_feats.shape
    cols = cotangent.shape[1]
    angles = source.shape[0]
    ext = capacity + 2 * GHOST
    chunk = depth // n_dom
    fused = chunk % 16 == 0
    src = source.reshape(angles // LANES, LANES)
    cos = cosine.reshape(angles // LANES, LANES)
    f32, bf16 = jnp.float32, jnp.bfloat16
    vmem = pl.BlockSpec(memory_space=pltpu.VMEM)
    outs = [jax.ShapeDtypeStruct((cols, capacity), bf16)]
    if fused:
        outs += [jax.ShapeDtypeStruct((chunk, cols), f32)] * 4
    else:
        outs += [jax.ShapeDtypeStruct((depth, 4 * cols), f32)]
    outs += [jax.ShapeDtypeStruct((1, cols), f32)]
    dma = pltpu.SemaphoreType.DMA
    scratch = [
        pltpu.VMEM((depth, 4 * cols), bf16),
        pltpu.VMEM((4 * cols, depth), bf16),
        pltpu.VMEM((depth, ext), bf16),
        pltpu.VMEM((2 * GHOST, depth), bf16),
        pltpu.VMEM((ext, angles), bf16),
        pltpu.VMEM((4 * cols, ext), bf16),
        pltpu.VMEM((4 * cols, angles), f32),
        pltpu.VMEM((cols, angles), f32),
        pltpu.VMEM((2 * cols, angles), bf16),
        pltpu.VMEM((depth, capacity + LANES), f32),
        pltpu.VMEM((n_wa, cols, capacity + LANES), bf16),
        pltpu.VMEM((n_wa - 1, cols, capacity + LANES), bf16),
        pltpu.VMEM((cols, LANES), bf16),
        pltpu.VMEM((2, cols, LANES), bf16),
        dma((2,)),
        dma((2,)),
        dma((n_wa - 1,)),
        dma((n_wa - 1,)),
        dma((2,)),
        dma((2,)),
        pltpu.VMEM((capacity, depth), bf16),
        pltpu.VMEM((cols, capacity), bf16),
        pltpu.SMEM((1,), jnp.int32),
        pltpu.VMEM((angles // LANES, LANES), jnp.int32),
        pltpu.VMEM((angles // LANES, LANES), f32),
        pltpu.VMEM((1, cols), f32),
        pltpu.VMEM((16, capacity), f32),
        dma((10,)),
    ]
    if fused:
        scratch += [
            pltpu.VMEM((depth, 4 * cols), f32),
            pltpu.VMEM((n_dom, chunk + 16, 4 * cols), bf16),
            pltpu.VMEM((n_dom - 1, chunk + 16, 4 * cols), bf16),
            dma((n_dom - 1,)),
            dma((n_dom - 1,)),
        ]
    results = pl.pallas_call(
        functools.partial(kernel, n_dom, n_wa, fused),
        out_shape=outs,
        in_specs=[pl.BlockSpec(memory_space=pltpu.HBM)] * 10,
        out_specs=[vmem] * len(outs),
        scratch_shapes=scratch,
        compiler_params=pltpu.CompilerParams(
            collective_id=0, has_side_effects=True, vmem_limit_bytes=67043328
        ),
        name="line_graph_backward",
    )(
        bond_feats,
        cotangent.T,
        bond_count,
        src,
        cos,
        w_source.T,
        w_target.T,
        w_message.T,
        w_self.T,
        gate_angle.reshape(1, cols),
    )
    if fused:
        bond_grad, one, two, four, five, gate = pl.pallas_call(
            put_out,
            out_shape=outs,
            in_specs=[vmem] * len(outs),
            out_specs=[pl.BlockSpec(memory_space=pltpu.HBM)] * len(outs),
            scratch_shapes=[dma((len(outs),))],
            name="put_out",
        )(*results)
        return bond_grad.T, one, two, four, five, gate.reshape(cols)
    bond_grad, grads, gate = results
    mine = lax.psum_scatter(grads, "dom", scatter_dimension=0, tiled=True)
    gate = lax.psum(gate.reshape(cols), "dom")
    one, four, two, five = (mine[:, i * cols : (i + 1) * cols] for i in range(4))
    return bond_grad.T, one, two, four, five, gate


def solution(mesh):
    return jax.shard_map(
        functools.partial(per_device, mesh.shape["dom"], mesh.shape["wa"]),
        mesh=mesh,
        in_specs=(
            P("dom", None),
            P("dom", "wa"),
            P("dom"),
            P("dom"),
            P("dom"),
            P(None, "wa"),
            P(None, "wa"),
            P(None, "wa"),
            P(None, "wa"),
            P("wa"),
        ),
        out_specs=(
            P("dom", "wa"),
            P("dom", "wa"),
            P("dom", "wa"),
            P("dom", "wa"),
            P("dom", "wa"),
            P("wa"),
        ),
        check_vma=False,
    )
```

```python
import functools

import jax
import jax.numpy as jnp
from jax import lax
from jax.experimental import pallas as pl
from jax.experimental.pallas import tpu as pltpu
from jax.sharding import PartitionSpec as P

ARITY = 12
GHOST = 32
MESH = pl.DeviceIdType.MESH
LANES = 128

epsilon = 1e-06

NT = (((1,), (1,)), ((), ()))


def dot(a, b):
    return jnp.dot(a, b, preferred_element_type=jnp.float32)


def dot_nt(a, b):
    return lax.dot_general(a, b, NT, preferred_element_type=jnp.float32)


def split(values):
    high = values.astype(jnp.bfloat16)
    low = (values - high.astype(jnp.float32)).astype(jnp.bfloat16)
    return high, low


def flipped(values):
    return values.astype(jnp.float32).T


def slot_major(src, cos, capacity):
    rows = src.shape[0]
    c_hi = cos.astype(jnp.bfloat16).astype(jnp.float32)
    parts = [(src >> 4).astype(jnp.float32), (src & 15).astype(jnp.float32), c_hi, cos - c_hi]
    a = lax.broadcasted_iota(jnp.int32, (LANES, 4 * LANES), 0)
    z = lax.broadcasted_iota(jnp.int32, (LANES, 4 * LANES), 1)
    turn = (8 * ARITY) * (z // LANES)
    mirror = jnp.where(a == (LANES - 1 + turn - z) % LANES, 1.0, 0.0).astype(jnp.bfloat16)
    mixed = dot(jnp.concatenate(parts, axis=0).astype(jnp.bfloat16), mirror)
    packed = jnp.concatenate(
        [
            jnp.concatenate(
                [mixed[i * rows : (i + 1) * rows, m * LANES : (m + 1) * LANES] for m in range(4)], axis=0
            )
            for i in range(4)
        ],
        axis=1,
    ).astype(jnp.bfloat16)
    b = lax.broadcasted_iota(jnp.int32, (capacity, 4 * rows), 0)
    q = lax.broadcasted_iota(jnp.int32, (capacity, 4 * rows), 1)
    want = ((b // 8) % 4) * rows + (ARITY * b) // LANES
    x0 = dot(jnp.where(q == want, 1.0, 0.0).astype(jnp.bfloat16), packed)
    x1 = dot(jnp.where(q == want + 1, 1.0, 0.0).astype(jnp.bfloat16), packed)
    bb = lax.broadcasted_iota(jnp.int32, (capacity, LANES), 0)
    p = lax.broadcasted_iota(jnp.int32, (capacity, LANES), 1)
    at = (LANES - 1 + 8 * ARITY * ((bb // 8) % 4) - p) % LANES
    first = at >= (ARITY * bb) % LANES
    def finish(v0, v1):
        v = jnp.where(first, v0, v1).reshape(capacity // 8, 8, LANES)
        v = pltpu.roll(v, 0, 2, stride=ARITY, stride_axis=1).reshape(capacity, LANES)
        return v.T[LANES - 16 :]
    s = finish(x0[:, :LANES] * 16.0 + x0[:, LANES:2*LANES], x1[:, :LANES] * 16.0 + x1[:, LANES:2*LANES])
    c = finish(x0[:, 2*LANES:3*LANES] + x0[:, 3*LANES:], x1[:, 2*LANES:3*LANES] + x1[:, 3*LANES:])
    return s, c


def kernel(
    n_dom,
    n_wa,
    fused,
    h_hbm,
    cot_hbm,
    count_hbm,
    src_hbm,
    cos_hbm,
    ws_hbm,
    wt_hbm,
    wm_hbm,
    wf_hbm,
    ga_hbm,
    bond_out,
    *refs,
):
    if fused:
        (g1_out, g2_out, g4_out, g5_out, gg_out) = refs[:5]
        refs = refs[5:]
    else:
        (g_out, gg_out) = refs[:2]
        refs = refs[2:]
    (
        wcat,
        wcat_t,
        h_t,
        gh,
        hot,
        table,
        picked,
        sig_s,
        dcol,
        own_w,
        wbuf,
        wrecv,
        gsend,
        grecv2,
        halo_send,
        halo_recv,
        wsend_sem,
        wrecv_sem,
        nsend_sem,
        nrecv_sem,
        h_ref,
        cot_ref,
        count_ref,
        src_ref,
        cosine_ref,
        ga_ref,
        cos_ref,
        in_sem,
    ) = refs[:28]
    if fused:
        (
            g_full,
            gbuf,
            grecv,
            gsend_sem,
            grecv_sem,
            tbuf,
            trecv,
            tsend_sem,
            trecv_sem,
        ) = refs[28:]
    dom = lax.axis_index("dom")
    wa = lax.axis_index("wa")
    capacity, depth = h_ref.shape
    cols = cot_ref.shape[0]
    up = (lax.rem(dom + 1, n_dom), wa)
    down = (lax.rem(dom + n_dom - 1, n_dom), wa)
    doms = range(1, n_dom) if fused else (1, n_dom - 1)

    barrier = pltpu.get_barrier_semaphore()
    for k in doms:
        pl.semaphore_signal(
            barrier, inc=1, device_id=(lax.rem(dom + k, n_dom), wa), device_id_type=MESH
        )
    for k in range(1, n_wa):
        side = lax.rem(wa + k, n_wa)
        for at in (dom, up[0], down[0]):
            pl.semaphore_signal(barrier, inc=1, device_id=(at, side), device_id_type=MESH)
    loads = []
    pairs = [
        (src_hbm, src_ref),
        (cos_hbm, cosine_ref),
        (h_hbm, h_ref),
        (count_hbm, count_ref),
        (cot_hbm, cot_ref),
        (ga_hbm, ga_ref),
    ]
    for i, w in enumerate((ws_hbm, wm_hbm, wt_hbm, wf_hbm)):
        pairs.append((w, wcat_t.at[pl.ds(i * cols, cols), :]))
    for i, (ours, to) in enumerate(pairs):
        copy = pltpu.make_async_copy(ours, to, in_sem.at[i])
        copy.start()
        loads.append(copy)
    pl.semaphore_wait(barrier, len(doms) + 3 * (n_wa - 1))

    to_up = pltpu.make_async_remote_copy(
        src_ref=h_hbm.at[pl.ds(capacity - GHOST, GHOST), :],
        dst_ref=gh.at[pl.ds(0, GHOST), :],
        send_sem=halo_send.at[0],
        recv_sem=halo_recv.at[0],
        device_id=up,
        device_id_type=MESH,
    )
    to_down = pltpu.make_async_remote_copy(
        src_ref=h_hbm.at[pl.ds(0, GHOST), :],
        dst_ref=gh.at[pl.ds(GHOST, GHOST), :],
        send_sem=halo_send.at[1],
        recv_sem=halo_recv.at[1],
        device_id=down,
        device_id_type=MESH,
    )
    to_up.start()
    to_down.start()

    loads[0].wait()
    loads[1].wait()
    sources, cosines = slot_major(src_ref[...], cosine_ref[...], capacity)
    cos_ref[...] = cosines

    ext = capacity + 2 * GHOST
    row_id = (
        lax.broadcasted_iota(jnp.int32, (capacity, capacity), 0)
        .astype(jnp.float32)
        .astype(jnp.bfloat16)
    )
    one = jnp.ones((), jnp.bfloat16)
    zero = jnp.zeros((), jnp.bfloat16)
    for j in range(ARITY):
        s = sources[15 - j : 16 - j, :]
        after = s >= capacity + GHOST
        own_row = jnp.where((s < GHOST) | after, 512.0, s - GHOST)
        side = jnp.where(s < GHOST, s, jnp.where(after, s - capacity, 512.0))
        here = pl.ds(j * capacity, capacity)
        hot[:capacity, here] = jnp.where(row_id == own_row.astype(jnp.bfloat16), one, zero)
        hot[capacity:, here] = jnp.where(
            row_id[: 2 * GHOST] == side.astype(jnp.bfloat16), one, zero
        )
    for copy in loads[2:]:
        copy.wait()
    h_t[:, :capacity] = flipped(h_ref[...]).astype(jnp.bfloat16)
    wcat[...] = flipped(wcat_t[...]).astype(jnp.bfloat16)
    proj = dot_nt(wcat_t[...], h_ref[...])
    lane = lax.broadcasted_iota(jnp.int32, (1, capacity), 1)
    count = count_ref[...]
    live = jnp.where(
        (lane < count - GHOST) | (lane >= capacity - GHOST), 1.0, 0.0
    ).astype(jnp.float32)
    cot_live = cot_ref[...].astype(jnp.float32) * live
    angle = jnp.broadcast_to(ga_ref[...], (LANES, cols)).T
    high, low = split(proj[: 2 * cols])
    table[: 2 * cols, :capacity] = high
    table[2 * cols :, :capacity] = low

    to_up.wait()
    to_down.wait()
    proj_g = dot_nt(wcat_t[: 2 * cols, :], gh[...])
    high, low = split(proj_g)
    table[: 2 * cols, capacity:] = high
    table[2 * cols :, capacity:] = low
    h_t[:, capacity:] = flipped(gh[...]).astype(jnp.bfloat16)

    picked[...] = dot(table[...], hot[...])

    parts_z = []
    parts_t = []
    gate_sum = jnp.zeros((cols, LANES), jnp.float32)
    for half in range(capacity // LANES):
        at = half * LANES
        q2 = proj[2 * cols : 3 * cols, at : at + LANES]
        base = proj[3 * cols :, at : at + LANES]
        lv = live[:, at : at + LANES]
        numer = jnp.zeros((cols, LANES), jnp.float32)
        denom = jnp.zeros((cols, LANES), jnp.float32)
        for j in range(ARITY):
            here = pl.ds(j * capacity + at, LANES)
            p1 = picked[0:cols, here] + picked[2 * cols : 3 * cols, here]
            p4 = picked[cols : 2 * cols, here] + picked[3 * cols :, here]
            pre = p1 + q2 + cos_ref[15 - j : 16 - j, at : at + LANES] * angle
            sig = jax.nn.sigmoid(pre)
            sig_s[:, here] = sig
            picked[cols : 2 * cols, here] = p4
            numer = numer + sig * p4
            denom = denom + sig
        inverse = 1.0 / (denom * lv + epsilon)
        agg = numer * lv * inverse
        z = base + agg
        sz = jax.nn.sigmoid(z)
        dz = cot_live[:, at : at + LANES] * (sz * (1.0 + z * (1.0 - sz)))
        dnum = dz * inverse
        dq2 = jnp.zeros((cols, LANES), jnp.float32)
        for j in range(ARITY):
            here = pl.ds(j * capacity + at, LANES)
            sig = sig_s[:, here]
            dmsg = sig * dnum
            dpre = dmsg * (picked[cols : 2 * cols, here] - agg) * (1.0 - sig)
            dq2 = dq2 + dpre
            gate_sum = gate_sum + cos_ref[15 - j : 16 - j, at : at + LANES] * dpre
            dcol[:cols, here] = dpre.astype(jnp.bfloat16)
            dcol[cols:, here] = dmsg.astype(jnp.bfloat16)
        parts_z.append(dz.astype(jnp.bfloat16))
        parts_t.append(dq2.astype(jnp.bfloat16))

    high, low = split(gate_sum)
    ones = jnp.ones((16, LANES), jnp.bfloat16)
    gate_row = (dot_nt(ones, high) + dot_nt(ones, low))[0:1]
    gcopies = []
    if fused:
        tbuf[:, :cols] = gate_row
        tbuf[:, cols:] = jnp.zeros((1, LANES - cols), jnp.float32)
        for k in range(1, n_dom):
            copy = pltpu.make_async_remote_copy(
                src_ref=tbuf,
                dst_ref=trecv.at[k - 1],
                send_sem=tsend_sem.at[k - 1],
                recv_sem=trecv_sem.at[k - 1],
                device_id=(lax.rem(dom + k, n_dom), wa),
                device_id_type=MESH,
            )
            copy.start()
            gcopies.append(copy)

    dghost = dot_nt(dcol[...], hot[capacity:, :]).astype(jnp.bfloat16)
    whole_g = dot(wcat[:, : 2 * cols], dghost).astype(jnp.bfloat16)
    whole_g = jnp.concatenate(
        [whole_g, jnp.zeros((depth, LANES - 2 * GHOST), jnp.bfloat16)], axis=1
    )
    for c in range(n_wa):
        gsend[c] = whole_g[c * cols : (c + 1) * cols]
    ncopies = []
    for k in range(n_wa):
        side = lax.rem(wa + k, n_wa)
        for i, to in enumerate((up[0], down[0])):
            copy = pltpu.make_async_remote_copy(
                src_ref=gsend.at[side],
                dst_ref=grecv2.at[i, k],
                send_sem=nsend_sem.at[i, k],
                recv_sem=nrecv_sem.at[i, k],
                device_id=(to, side),
                device_id_type=MESH,
            )
            copy.start()
            ncopies.append(copy)

    rows = dot_nt(dcol[...], hot[:capacity, :]).astype(jnp.bfloat16)
    dcat = jnp.concatenate(
        [rows, jnp.concatenate(parts_t, axis=1), jnp.concatenate(parts_z, axis=1)], axis=0
    )
    grads = dot_nt(h_t[:, :capacity], dcat)
    grads_g = dot_nt(h_t[:, capacity:], dghost)
    grads = jnp.concatenate([grads[:, : 2 * cols] + grads_g, grads[:, 2 * cols :]], axis=1)
    if fused:
        chunk = depth // n_dom
        g_full[...] = grads
        for i in range(n_dom):
            gbuf[i] = grads[i * chunk : (i + 1) * chunk].astype(jnp.bfloat16)
        for k in range(1, n_dom):
            to = lax.rem(dom + k, n_dom)
            copy = pltpu.make_async_remote_copy(
                src_ref=gbuf.at[to],
                dst_ref=grecv.at[k - 1],
                send_sem=gsend_sem.at[k - 1],
                recv_sem=grecv_sem.at[k - 1],
                device_id=(to, wa),
                device_id_type=MESH,
            )
            copy.start()
            gcopies.append(copy)
    else:
        g_out[...] = grads
        gg_out[...] = gate_row

    whole = dot(wcat[...], dcat)
    own_w[...] = whole
    for c in range(n_wa):
        wbuf[c] = whole[c * cols : (c + 1) * cols].astype(jnp.bfloat16)
    wcopies = []
    for k in range(1, n_wa):
        to = lax.rem(wa + k, n_wa)
        copy = pltpu.make_async_remote_copy(
            src_ref=wbuf.at[to],
            dst_ref=wrecv.at[k - 1],
            send_sem=wsend_sem.at[k - 1],
            recv_sem=wrecv_sem.at[k - 1],
            device_id=(dom, to),
            device_id_type=MESH,
        )
        copy.start()
        wcopies.append(copy)

    for copy in wcopies:
        copy.wait()
    mine = pl.ds(pl.multiple_of(wa * cols, cols), cols)
    total = own_w[mine, :]
    for k in range(n_wa - 1):
        total = total + wrecv[k].astype(jnp.float32)
    own = total + cot_live
    if fused:
        for copy in gcopies:
            copy.wait()
        acc = g_full[pl.ds(pl.multiple_of(dom * chunk, chunk), chunk), :]
        gate = gate_row
        for k in range(n_dom - 1):
            acc = acc + grecv[k].astype(jnp.float32)
            gate = gate + trecv[k][:, :cols]
        g1_out[...] = acc[:, :cols]
        g4_out[...] = acc[:, cols : 2 * cols]
        g2_out[...] = acc[:, 2 * cols : 3 * cols]
        g5_out[...] = acc[:, 3 * cols :]
        gg_out[...] = gate

    for copy in ncopies:
        copy.wait()
    lane_t = lax.broadcasted_iota(jnp.int32, (cols, LANES), 1)
    below = jnp.zeros((cols, LANES), jnp.float32)
    above = jnp.zeros((cols, LANES), jnp.float32)
    for k in range(n_wa):
        below = below + grecv2[0, k].astype(jnp.float32)
        above = above + grecv2[1, k].astype(jnp.float32)
    below = pltpu.roll(below, LANES - GHOST, 1)
    above = pltpu.roll(above, LANES - GHOST, 1)
    first = own[:, :LANES] + jnp.where(lane_t < GHOST, below, 0.0)
    last = own[:, capacity - LANES :] + jnp.where(lane_t >= LANES - GHOST, above, 0.0)
    result = jnp.concatenate([first, own[:, LANES : capacity - LANES], last], axis=1) if capacity > 2 * LANES else jnp.concatenate([first, last], axis=1)
    bond_out[...] = result.astype(jnp.bfloat16)


def put_out(*refs):
    count = len(refs) // 2
    sem = refs[-1]
    copies = [
        pltpu.make_async_copy(refs[i], refs[count + i], sem.at[i]) for i in range(count)
    ]
    for copy in copies:
        copy.start()
    for copy in copies:
        copy.wait()


def per_device(
    n_dom,
    n_wa,
    bond_feats,
    cotangent,
    bond_count,
    source,
    cosine,
    w_source,
    w_target,
    w_message,
    w_self,
    gate_angle,
):
    capacity, depth = bond_feats.shape
    cols = cotangent.shape[1]
    angles = source.shape[0]
    ext = capacity + 2 * GHOST
    chunk = depth // n_dom
    fused = chunk % 16 == 0
    src = source.reshape(angles // LANES, LANES)
    cos = cosine.reshape(angles // LANES, LANES)
    f32, bf16 = jnp.float32, jnp.bfloat16
    vmem = pl.BlockSpec(memory_space=pltpu.VMEM)
    outs = [jax.ShapeDtypeStruct((cols, capacity), bf16)]
    if fused:
        outs += [jax.ShapeDtypeStruct((chunk, cols), f32)] * 4
    else:
        outs += [jax.ShapeDtypeStruct((depth, 4 * cols), f32)]
    outs += [jax.ShapeDtypeStruct((1, cols), f32)]
    dma = pltpu.SemaphoreType.DMA
    scratch = [
        pltpu.VMEM((depth, 4 * cols), bf16),
        pltpu.VMEM((4 * cols, depth), bf16),
        pltpu.VMEM((depth, ext), bf16),
        pltpu.VMEM((2 * GHOST, depth), bf16),
        pltpu.VMEM((ext, angles), bf16),
        pltpu.VMEM((4 * cols, ext), bf16),
        pltpu.VMEM((4 * cols, angles), f32),
        pltpu.VMEM((cols, angles), f32),
        pltpu.VMEM((2 * cols, angles), bf16),
        pltpu.VMEM((depth, capacity), f32),
        pltpu.VMEM((n_wa, cols, capacity), bf16),
        pltpu.VMEM((n_wa - 1, cols, capacity), bf16),
        pltpu.VMEM((n_wa, cols, LANES), bf16),
        pltpu.VMEM((2, n_wa, cols, LANES), bf16),
        dma((2,)),
        dma((2,)),
        dma((n_wa - 1,)),
        dma((n_wa - 1,)),
        dma((2, n_wa)),
        dma((2, n_wa)),
        pltpu.VMEM((capacity, depth), bf16),
        pltpu.VMEM((cols, capacity), bf16),
        pltpu.VMEM((1, 1), jnp.int32),
        pltpu.VMEM((angles // LANES, LANES), jnp.int32),
        pltpu.VMEM((angles // LANES, LANES), f32),
        pltpu.VMEM((1, cols), f32),
        pltpu.VMEM((16, capacity), f32),
        dma((10,)),
    ]
    if fused:
        scratch += [
            pltpu.VMEM((depth, 4 * cols), f32),
            pltpu.VMEM((n_dom, chunk, 4 * cols), bf16),
            pltpu.VMEM((n_dom - 1, chunk, 4 * cols), bf16),
            dma((n_dom - 1,)),
            dma((n_dom - 1,)),
            pltpu.VMEM((1, LANES), f32),
            pltpu.VMEM((n_dom - 1, 1, LANES), f32),
            dma((n_dom - 1,)),
            dma((n_dom - 1,)),
        ]
    results = pl.pallas_call(
        functools.partial(kernel, n_dom, n_wa, fused),
        out_shape=outs,
        in_specs=[pl.BlockSpec(memory_space=pltpu.HBM)] * 10,
        out_specs=[vmem] * len(outs),
        scratch_shapes=scratch,
        compiler_params=pltpu.CompilerParams(
            collective_id=0, has_side_effects=True, vmem_limit_bytes=67043328
        ),
        name="line_graph_backward",
    )(
        bond_feats,
        cotangent.T,
        bond_count.reshape(1, 1),
        src,
        cos,
        w_source.T,
        w_target.T,
        w_message.T,
        w_self.T,
        gate_angle.reshape(1, cols),
    )
    if fused:
        bond_grad, one, two, four, five, gate = pl.pallas_call(
            put_out,
            out_shape=outs,
            in_specs=[vmem] * len(outs),
            out_specs=[pl.BlockSpec(memory_space=pltpu.HBM)] * len(outs),
            scratch_shapes=[dma((len(outs),))],
            name="put_out",
        )(*results)
        return bond_grad.T, one, two, four, five, gate.reshape(cols)
    bond_grad, grads, gate = results
    mine = lax.psum_scatter(grads, "dom", scatter_dimension=0, tiled=True)
    gate = lax.psum(gate.reshape(cols), "dom")
    one, four, two, five = (mine[:, i * cols : (i + 1) * cols] for i in range(4))
    return bond_grad.T, one, two, four, five, gate


def solution(mesh):
    return jax.shard_map(
        functools.partial(per_device, mesh.shape["dom"], mesh.shape["wa"]),
        mesh=mesh,
        in_specs=(
            P("dom", None),
            P("dom", "wa"),
            P("dom"),
            P("dom"),
            P("dom"),
            P(None, "wa"),
            P(None, "wa"),
            P(None, "wa"),
            P(None, "wa"),
            P("wa"),
        ),
        out_specs=(
            P("dom", "wa"),
            P("dom", "wa"),
            P("dom", "wa"),
            P("dom", "wa"),
            P("dom", "wa"),
            P("wa"),
        ),
        check_vma=False,
    )
```

```python
import functools

import jax
import jax.numpy as jnp
from jax import lax
from jax.experimental import pallas as pl
from jax.experimental.pallas import tpu as pltpu
from jax.sharding import PartitionSpec as P

ARITY = 12
GHOST = 32
MESH = pl.DeviceIdType.MESH
LANES = 128

epsilon = 1e-06

NT = (((1,), (1,)), ((), ()))


def dot(a, b):
    return jnp.dot(a, b, preferred_element_type=jnp.float32)


def dot_nt(a, b):
    return lax.dot_general(a, b, NT, preferred_element_type=jnp.float32)


def split(values):
    high = values.astype(jnp.bfloat16)
    low = (values - high.astype(jnp.float32)).astype(jnp.bfloat16)
    return high, low


def flipped(values):
    return values.astype(jnp.float32).T


def slot_major(src, cos, capacity):
    rows = src.shape[0]
    c_hi = cos.astype(jnp.bfloat16).astype(jnp.float32)
    parts = [(src >> 4).astype(jnp.float32), (src & 15).astype(jnp.float32), c_hi, cos - c_hi]
    a = lax.broadcasted_iota(jnp.int32, (LANES, 4 * LANES), 0)
    z = lax.broadcasted_iota(jnp.int32, (LANES, 4 * LANES), 1)
    turn = (8 * ARITY) * (z // LANES)
    mirror = jnp.where(a == (LANES - 1 + turn - z) % LANES, 1.0, 0.0).astype(jnp.bfloat16)
    mixed = dot(jnp.concatenate(parts, axis=0).astype(jnp.bfloat16), mirror)
    packed = jnp.concatenate(
        [
            jnp.concatenate(
                [mixed[i * rows : (i + 1) * rows, m * LANES : (m + 1) * LANES] for m in range(4)], axis=0
            )
            for i in range(4)
        ],
        axis=1,
    ).astype(jnp.bfloat16)
    b = lax.broadcasted_iota(jnp.int32, (capacity, 4 * rows), 0)
    q = lax.broadcasted_iota(jnp.int32, (capacity, 4 * rows), 1)
    want = ((b // 8) % 4) * rows + (ARITY * b) // LANES
    x0 = dot(jnp.where(q == want, 1.0, 0.0).astype(jnp.bfloat16), packed)
    x1 = dot(jnp.where(q == want + 1, 1.0, 0.0).astype(jnp.bfloat16), packed)
    bb = lax.broadcasted_iota(jnp.int32, (capacity, LANES), 0)
    p = lax.broadcasted_iota(jnp.int32, (capacity, LANES), 1)
    at = (LANES - 1 + 8 * ARITY * ((bb // 8) % 4) - p) % LANES
    first = at >= (ARITY * bb) % LANES
    def finish(v0, v1):
        v = jnp.where(first, v0, v1).reshape(capacity // 8, 8, LANES)
        v = pltpu.roll(v, 0, 2, stride=ARITY, stride_axis=1).reshape(capacity, LANES)
        return v.T[LANES - 16 :]
    s = finish(x0[:, :LANES] * 16.0 + x0[:, LANES:2*LANES], x1[:, :LANES] * 16.0 + x1[:, LANES:2*LANES])
    c = finish(x0[:, 2*LANES:3*LANES] + x0[:, 3*LANES:], x1[:, 2*LANES:3*LANES] + x1[:, 3*LANES:])
    return s, c


def packed_sides(values):
    count = LANES // GHOST
    rows = values.shape[0] // count
    place = lax.broadcasted_iota(jnp.int32, (rows, LANES), 1) // GHOST
    sides = []
    for side in range(2):
        out = None
        for q in range(count):
            piece = values[q * rows : (q + 1) * rows]
            turn = (GHOST * (q - side)) % LANES
            piece = pltpu.roll(piece, turn, 1) if turn else piece
            out = piece if out is None else jnp.where(place == q, piece, out)
        sides.append(out)
    return sides


def unpacked(values, lane_block):
    count = LANES // GHOST
    place = lax.broadcasted_iota(jnp.int32, values.shape, 1) // GHOST
    pieces = []
    for q in range(count):
        turn = (GHOST * (lane_block - q)) % LANES
        piece = pltpu.roll(values, turn, 1) if turn else values
        pieces.append(jnp.where(place == lane_block, piece, 0.0))
    return jnp.concatenate(pieces, axis=0)


def kernel(
    n_dom,
    n_wa,
    fused,
    h_hbm,
    cot_hbm,
    count_hbm,
    src_hbm,
    cos_hbm,
    ws_hbm,
    wt_hbm,
    wm_hbm,
    wf_hbm,
    ga_hbm,
    bond_out,
    *refs,
):
    if fused:
        (g1_out, g2_out, g4_out, g5_out, gg_out) = refs[:5]
        refs = refs[5:]
    else:
        (g_out, gg_out) = refs[:2]
        refs = refs[2:]
    (
        wcat,
        wcat_t,
        h_t,
        gh,
        hot,
        table,
        picked,
        sig_s,
        dcol,
        own_w,
        wbuf,
        wrecv,
        gsend,
        grecv2,
        halo_send,
        halo_recv,
        wsend_sem,
        wrecv_sem,
        nsend_sem,
        nrecv_sem,
        h_ref,
        cot_ref,
        count_ref,
        src_ref,
        cosine_ref,
        ga_ref,
        cos_ref,
        in_sem,
    ) = refs[:28]
    if fused:
        (
            g_full,
            gbuf,
            grecv,
            gsend_sem,
            grecv_sem,
            tbuf,
            trecv,
            tsend_sem,
            trecv_sem,
        ) = refs[28:]
    dom = lax.axis_index("dom")
    wa = lax.axis_index("wa")
    capacity, depth = h_ref.shape
    cols = cot_ref.shape[0]
    up = (lax.rem(dom + 1, n_dom), wa)
    down = (lax.rem(dom + n_dom - 1, n_dom), wa)
    doms = range(1, n_dom) if fused else (1, n_dom - 1)

    barrier = pltpu.get_barrier_semaphore()
    for k in doms:
        pl.semaphore_signal(
            barrier, inc=1, device_id=(lax.rem(dom + k, n_dom), wa), device_id_type=MESH
        )
    for k in range(1, n_wa):
        side = lax.rem(wa + k, n_wa)
        for at in (dom, up[0], down[0]):
            pl.semaphore_signal(barrier, inc=1, device_id=(at, side), device_id_type=MESH)
    loads = []
    pairs = [
        (src_hbm, src_ref),
        (cos_hbm, cosine_ref),
        (h_hbm, h_ref),
        (count_hbm, count_ref),
        (cot_hbm, cot_ref),
        (ga_hbm, ga_ref),
    ]
    for i, w in enumerate((ws_hbm, wm_hbm, wt_hbm, wf_hbm)):
        pairs.append((w, wcat_t.at[pl.ds(i * cols, cols), :]))
    for i, (ours, to) in enumerate(pairs):
        copy = pltpu.make_async_copy(ours, to, in_sem.at[i])
        copy.start()
        loads.append(copy)
    pl.semaphore_wait(barrier, len(doms) + 3 * (n_wa - 1))

    to_up = pltpu.make_async_remote_copy(
        src_ref=h_hbm.at[pl.ds(capacity - GHOST, GHOST), :],
        dst_ref=gh.at[pl.ds(0, GHOST), :],
        send_sem=halo_send.at[0],
        recv_sem=halo_recv.at[0],
        device_id=up,
        device_id_type=MESH,
    )
    to_down = pltpu.make_async_remote_copy(
        src_ref=h_hbm.at[pl.ds(0, GHOST), :],
        dst_ref=gh.at[pl.ds(GHOST, GHOST), :],
        send_sem=halo_send.at[1],
        recv_sem=halo_recv.at[1],
        device_id=down,
        device_id_type=MESH,
    )
    to_up.start()
    to_down.start()

    loads[0].wait()
    loads[1].wait()
    sources, cosines = slot_major(src_ref[...], cosine_ref[...], capacity)
    cos_ref[...] = cosines

    ext = capacity + 2 * GHOST
    row_id = (
        lax.broadcasted_iota(jnp.int32, (capacity, capacity), 0)
        .astype(jnp.float32)
        .astype(jnp.bfloat16)
    )
    one = jnp.ones((), jnp.bfloat16)
    zero = jnp.zeros((), jnp.bfloat16)
    for j in range(ARITY):
        s = sources[15 - j : 16 - j, :]
        after = s >= capacity + GHOST
        own_row = jnp.where((s < GHOST) | after, 512.0, s - GHOST)
        side = jnp.where(s < GHOST, s, jnp.where(after, s - capacity, 512.0))
        here = pl.ds(j * capacity, capacity)
        hot[:capacity, here] = jnp.where(row_id == own_row.astype(jnp.bfloat16), one, zero)
        hot[capacity:, here] = jnp.where(
            row_id[: 2 * GHOST] == side.astype(jnp.bfloat16), one, zero
        )
    for copy in loads[2:]:
        copy.wait()
    h_t[:, :capacity] = flipped(h_ref[...]).astype(jnp.bfloat16)
    wcat[...] = flipped(wcat_t[...]).astype(jnp.bfloat16)
    proj = dot_nt(wcat_t[...], h_ref[...])
    lane = lax.broadcasted_iota(jnp.int32, (1, capacity), 1)
    count = count_ref[0]
    live = jnp.where(
        (lane < count - GHOST) | (lane >= capacity - GHOST), 1.0, 0.0
    ).astype(jnp.float32)
    cot_live = cot_ref[...].astype(jnp.float32) * live
    angle = jnp.broadcast_to(ga_ref[...], (LANES, cols)).T
    high, low = split(proj[: 2 * cols])
    table[: 2 * cols, :capacity] = high
    table[2 * cols :, :capacity] = low

    to_up.wait()
    to_down.wait()
    proj_g = dot_nt(wcat_t[: 2 * cols, :], gh[...])
    high, low = split(proj_g)
    table[: 2 * cols, capacity:] = high
    table[2 * cols :, capacity:] = low
    h_t[:, capacity:] = flipped(gh[...]).astype(jnp.bfloat16)

    picked[...] = dot(table[...], hot[...])

    parts_z = []
    parts_t = []
    gate_sum = jnp.zeros((cols, LANES), jnp.float32)
    for half in range(capacity // LANES):
        at = half * LANES
        q2 = proj[2 * cols : 3 * cols, at : at + LANES]
        base = proj[3 * cols :, at : at + LANES]
        lv = live[:, at : at + LANES]
        numer = jnp.zeros((cols, LANES), jnp.float32)
        denom = jnp.zeros((cols, LANES), jnp.float32)
        for j in range(ARITY):
            here = pl.ds(j * capacity + at, LANES)
            p1 = picked[0:cols, here] + picked[2 * cols : 3 * cols, here]
            p4 = picked[cols : 2 * cols, here] + picked[3 * cols :, here]
            pre = p1 + q2 + cos_ref[15 - j : 16 - j, at : at + LANES] * angle
            sig = jax.nn.sigmoid(pre)
            sig_s[:, here] = sig
            picked[cols : 2 * cols, here] = p4
            numer = numer + sig * p4
            denom = denom + sig
        inverse = 1.0 / (denom * lv + epsilon)
        agg = numer * lv * inverse
        z = base + agg
        sz = jax.nn.sigmoid(z)
        dz = cot_live[:, at : at + LANES] * (sz * (1.0 + z * (1.0 - sz)))
        dnum = dz * inverse
        dq2 = jnp.zeros((cols, LANES), jnp.float32)
        for j in range(ARITY):
            here = pl.ds(j * capacity + at, LANES)
            sig = sig_s[:, here]
            dmsg = sig * dnum
            dpre = dmsg * (picked[cols : 2 * cols, here] - agg) * (1.0 - sig)
            dq2 = dq2 + dpre
            gate_sum = gate_sum + cos_ref[15 - j : 16 - j, at : at + LANES] * dpre
            dcol[:cols, here] = dpre.astype(jnp.bfloat16)
            dcol[cols:, here] = dmsg.astype(jnp.bfloat16)
        parts_z.append(dz.astype(jnp.bfloat16))
        parts_t.append(dq2.astype(jnp.bfloat16))

    high, low = split(gate_sum)
    ones = jnp.ones((16, LANES), jnp.bfloat16)
    gate_row = (dot_nt(ones, high) + dot_nt(ones, low))[0:1]
    gcopies = []
    if fused:
        tbuf[:, :cols] = gate_row
        tbuf[:, cols:] = jnp.zeros((1, LANES - cols), jnp.float32)
        for k in range(1, n_dom):
            copy = pltpu.make_async_remote_copy(
                src_ref=tbuf,
                dst_ref=trecv.at[k - 1],
                send_sem=tsend_sem.at[k - 1],
                recv_sem=trecv_sem.at[k - 1],
                device_id=(lax.rem(dom + k, n_dom), wa),
                device_id_type=MESH,
            )
            copy.start()
            gcopies.append(copy)

    dghost = dot_nt(dcol[...], hot[capacity:, :]).astype(jnp.bfloat16)
    whole_g = dot(wcat[:, : 2 * cols], dghost)
    whole_g = jnp.concatenate(
        [whole_g, jnp.zeros((depth, LANES - 2 * GHOST), jnp.float32)], axis=1
    )
    for c in range(n_wa):
        before, after = packed_sides(whole_g[c * cols : (c + 1) * cols])
        gsend[0, c] = after.astype(jnp.bfloat16)
        gsend[1, c] = before.astype(jnp.bfloat16)
    ncopies = []
    for k in range(n_wa):
        side = lax.rem(wa + k, n_wa)
        for i, to in enumerate((up[0], down[0])):
            copy = pltpu.make_async_remote_copy(
                src_ref=gsend.at[i, side],
                dst_ref=grecv2.at[i, k],
                send_sem=nsend_sem.at[i, k],
                recv_sem=nrecv_sem.at[i, k],
                device_id=(to, side),
                device_id_type=MESH,
            )
            copy.start()
            ncopies.append(copy)

    rows = dot_nt(dcol[...], hot[:capacity, :]).astype(jnp.bfloat16)
    dcat = jnp.concatenate(
        [rows, jnp.concatenate(parts_t, axis=1), jnp.concatenate(parts_z, axis=1)], axis=0
    )
    grads = dot_nt(h_t[:, :capacity], dcat)
    grads_g = dot_nt(h_t[:, capacity:], dghost)
    grads = jnp.concatenate([grads[:, : 2 * cols] + grads_g, grads[:, 2 * cols :]], axis=1)
    if fused:
        chunk = depth // n_dom
        g_full[...] = grads
        for i in range(n_dom):
            gbuf[i] = grads[i * chunk : (i + 1) * chunk].astype(jnp.bfloat16)
        for k in range(1, n_dom):
            to = lax.rem(dom + k, n_dom)
            copy = pltpu.make_async_remote_copy(
                src_ref=gbuf.at[to],
                dst_ref=grecv.at[k - 1],
                send_sem=gsend_sem.at[k - 1],
                recv_sem=grecv_sem.at[k - 1],
                device_id=(to, wa),
                device_id_type=MESH,
            )
            copy.start()
            gcopies.append(copy)
    else:
        g_out[...] = grads
        gg_out[...] = gate_row

    whole = dot(wcat[...], dcat)
    own_w[...] = whole
    for c in range(n_wa):
        wbuf[c] = whole[c * cols : (c + 1) * cols].astype(jnp.bfloat16)
    wcopies = []
    for k in range(1, n_wa):
        to = lax.rem(wa + k, n_wa)
        copy = pltpu.make_async_remote_copy(
            src_ref=wbuf.at[to],
            dst_ref=wrecv.at[k - 1],
            send_sem=wsend_sem.at[k - 1],
            recv_sem=wrecv_sem.at[k - 1],
            device_id=(dom, to),
            device_id_type=MESH,
        )
        copy.start()
        wcopies.append(copy)

    for copy in wcopies:
        copy.wait()
    mine = pl.ds(pl.multiple_of(wa * cols, cols), cols)
    total = own_w[mine, :]
    for k in range(n_wa - 1):
        total = total + wrecv[k].astype(jnp.float32)
    own = total + cot_live
    if fused:
        for copy in gcopies:
            copy.wait()
        acc = g_full[pl.ds(pl.multiple_of(dom * chunk, chunk), chunk), :]
        gate = gate_row
        for k in range(n_dom - 1):
            acc = acc + grecv[k].astype(jnp.float32)
            gate = gate + trecv[k][:, :cols]
        g1_out[...] = acc[:, :cols]
        g4_out[...] = acc[:, cols : 2 * cols]
        g2_out[...] = acc[:, 2 * cols : 3 * cols]
        g5_out[...] = acc[:, 3 * cols :]
        gg_out[...] = gate

    for copy in ncopies:
        copy.wait()
    below = jnp.zeros(grecv2.shape[2:], jnp.float32)
    above = jnp.zeros(grecv2.shape[2:], jnp.float32)
    for k in range(n_wa):
        below = below + grecv2[0, k].astype(jnp.float32)
        above = above + grecv2[1, k].astype(jnp.float32)
    first = own[:, :LANES] + unpacked(below, 0)
    last = own[:, capacity - LANES :] + unpacked(above, LANES // GHOST - 1)
    result = jnp.concatenate([first, own[:, LANES : capacity - LANES], last], axis=1) if capacity > 2 * LANES else jnp.concatenate([first, last], axis=1)
    bond_out[...] = result.astype(jnp.bfloat16)


def put_out(*refs):
    count = len(refs) // 2
    sem = refs[-1]
    copies = [
        pltpu.make_async_copy(refs[i], refs[count + i], sem.at[i]) for i in range(count)
    ]
    for copy in copies:
        copy.start()
    for copy in copies:
        copy.wait()


def per_device(
    n_dom,
    n_wa,
    bond_feats,
    cotangent,
    bond_count,
    source,
    cosine,
    w_source,
    w_target,
    w_message,
    w_self,
    gate_angle,
):
    capacity, depth = bond_feats.shape
    cols = cotangent.shape[1]
    angles = source.shape[0]
    ext = capacity + 2 * GHOST
    chunk = depth // n_dom
    fused = chunk % 16 == 0
    src = source.reshape(angles // LANES, LANES)
    cos = cosine.reshape(angles // LANES, LANES)
    f32, bf16 = jnp.float32, jnp.bfloat16
    vmem = pl.BlockSpec(memory_space=pltpu.VMEM)
    outs = [jax.ShapeDtypeStruct((cols, capacity), bf16)]
    if fused:
        outs += [jax.ShapeDtypeStruct((chunk, cols), f32)] * 4
    else:
        outs += [jax.ShapeDtypeStruct((depth, 4 * cols), f32)]
    outs += [jax.ShapeDtypeStruct((1, cols), f32)]
    dma = pltpu.SemaphoreType.DMA
    scratch = [
        pltpu.VMEM((depth, 4 * cols), bf16),
        pltpu.VMEM((4 * cols, depth), bf16),
        pltpu.VMEM((depth, ext), bf16),
        pltpu.VMEM((2 * GHOST, depth), bf16),
        pltpu.VMEM((ext, angles), bf16),
        pltpu.VMEM((4 * cols, ext), bf16),
        pltpu.VMEM((4 * cols, angles), f32),
        pltpu.VMEM((cols, angles), f32),
        pltpu.VMEM((2 * cols, angles), bf16),
        pltpu.VMEM((depth, capacity), f32),
        pltpu.VMEM((n_wa, cols, capacity), bf16),
        pltpu.VMEM((n_wa - 1, cols, capacity), bf16),
        pltpu.VMEM((2, n_wa, cols * GHOST // LANES, LANES), bf16),
        pltpu.VMEM((2, n_wa, cols * GHOST // LANES, LANES), bf16),
        dma((2,)),
        dma((2,)),
        dma((n_wa - 1,)),
        dma((n_wa - 1,)),
        dma((2, n_wa)),
        dma((2, n_wa)),
        pltpu.VMEM((capacity, depth), bf16),
        pltpu.VMEM((cols, capacity), bf16),
        pltpu.SMEM((1,), jnp.int32),
        pltpu.VMEM((angles // LANES, LANES), jnp.int32),
        pltpu.VMEM((angles // LANES, LANES), f32),
        pltpu.VMEM((1, cols), f32),
        pltpu.VMEM((16, capacity), f32),
        dma((10,)),
    ]
    if fused:
        scratch += [
            pltpu.VMEM((depth, 4 * cols), f32),
            pltpu.VMEM((n_dom, chunk, 4 * cols), bf16),
            pltpu.VMEM((n_dom - 1, chunk, 4 * cols), bf16),
            dma((n_dom - 1,)),
            dma((n_dom - 1,)),
            pltpu.VMEM((1, LANES), f32),
            pltpu.VMEM((n_dom - 1, 1, LANES), f32),
            dma((n_dom - 1,)),
            dma((n_dom - 1,)),
        ]
    results = pl.pallas_call(
        functools.partial(kernel, n_dom, n_wa, fused),
        out_shape=outs,
        in_specs=[pl.BlockSpec(memory_space=pltpu.HBM)] * 10,
        out_specs=[vmem] * len(outs),
        scratch_shapes=scratch,
        compiler_params=pltpu.CompilerParams(
            collective_id=0, has_side_effects=True, vmem_limit_bytes=48 << 20
        ),
        name="line_graph_backward",
    )(
        *(
            operand
            if operand.size == 1
            else pltpu.with_memory_space_constraint(operand, pltpu.HBM)
            for operand in (
                bond_feats,
                cotangent.T,
                bond_count,
                src,
                cos,
                w_source.T,
                w_target.T,
                w_message.T,
                w_self.T,
                gate_angle.reshape(1, cols),
            )
        )
    )
    if fused:
        bond_grad, one, two, four, five, gate = pl.pallas_call(
            put_out,
            out_shape=outs,
            in_specs=[vmem] * len(outs),
            out_specs=[pl.BlockSpec(memory_space=pltpu.HBM)] * len(outs),
            scratch_shapes=[dma((len(outs),))],
            name="put_out",
        )(*(pltpu.with_memory_space_constraint(r, pltpu.VMEM) for r in results))
        return bond_grad.T, one, two, four, five, gate.reshape(cols)
    bond_grad, grads, gate = results
    mine = lax.psum_scatter(grads, "dom", scatter_dimension=0, tiled=True)
    gate = lax.psum(gate.reshape(cols), "dom")
    one, four, two, five = (mine[:, i * cols : (i + 1) * cols] for i in range(4))
    return bond_grad.T, one, two, four, five, gate


def solution(mesh):
    return jax.shard_map(
        functools.partial(per_device, mesh.shape["dom"], mesh.shape["wa"]),
        mesh=mesh,
        in_specs=(
            P("dom", None),
            P("dom", "wa"),
            P("dom"),
            P("dom"),
            P("dom"),
            P(None, "wa"),
            P(None, "wa"),
            P(None, "wa"),
            P(None, "wa"),
            P("wa"),
        ),
        out_specs=(
            P("dom", "wa"),
            P("dom", "wa"),
            P("dom", "wa"),
            P("dom", "wa"),
            P("dom", "wa"),
            P("wa"),
        ),
        check_vma=False,
    )
```

```python
import functools

import jax
import jax.numpy as jnp
from jax import lax
from jax.experimental import pallas as pl
from jax.experimental.pallas import tpu as pltpu
from jax.sharding import PartitionSpec as P

ARITY = 12
GHOST = 32
MESH = pl.DeviceIdType.MESH
LANES = 128

epsilon = 1e-06

NT = (((1,), (1,)), ((), ()))


def dot(a, b):
    return jnp.dot(a, b, preferred_element_type=jnp.float32)


def dot_nt(a, b):
    return lax.dot_general(a, b, NT, preferred_element_type=jnp.float32)


def split(values):
    high = values.astype(jnp.bfloat16)
    low = (values - high.astype(jnp.float32)).astype(jnp.bfloat16)
    return high, low


def flipped(values):
    return values.astype(jnp.float32).T


def slot_major(src, cos, capacity):
    rows = src.shape[0]
    c_hi = cos.astype(jnp.bfloat16).astype(jnp.float32)
    parts = [(src >> 4).astype(jnp.float32), (src & 15).astype(jnp.float32), c_hi, cos - c_hi]
    a = lax.broadcasted_iota(jnp.int32, (LANES, 4 * LANES), 0)
    z = lax.broadcasted_iota(jnp.int32, (LANES, 4 * LANES), 1)
    turn = (8 * ARITY) * (z // LANES)
    mirror = jnp.where(a == (LANES - 1 + turn - z) % LANES, 1.0, 0.0).astype(jnp.bfloat16)
    mixed = dot(jnp.concatenate(parts, axis=0).astype(jnp.bfloat16), mirror)
    packed = jnp.concatenate(
        [
            jnp.concatenate(
                [mixed[i * rows : (i + 1) * rows, m * LANES : (m + 1) * LANES] for m in range(4)], axis=0
            )
            for i in range(4)
        ],
        axis=1,
    ).astype(jnp.bfloat16)
    b = lax.broadcasted_iota(jnp.int32, (capacity, 4 * rows), 0)
    q = lax.broadcasted_iota(jnp.int32, (capacity, 4 * rows), 1)
    want = ((b // 8) % 4) * rows + (ARITY * b) // LANES
    x0 = dot(jnp.where(q == want, 1.0, 0.0).astype(jnp.bfloat16), packed)
    x1 = dot(jnp.where(q == want + 1, 1.0, 0.0).astype(jnp.bfloat16), packed)
    bb = lax.broadcasted_iota(jnp.int32, (capacity, LANES), 0)
    p = lax.broadcasted_iota(jnp.int32, (capacity, LANES), 1)
    at = (LANES - 1 + 8 * ARITY * ((bb // 8) % 4) - p) % LANES
    first = at >= (ARITY * bb) % LANES
    def finish(v0, v1):
        v = jnp.where(first, v0, v1).reshape(capacity // 8, 8, LANES)
        v = pltpu.roll(v, 0, 2, stride=ARITY, stride_axis=1).reshape(capacity, LANES)
        return v.T[LANES - 16 :]
    s = finish(x0[:, :LANES] * 16.0 + x0[:, LANES:2*LANES], x1[:, :LANES] * 16.0 + x1[:, LANES:2*LANES])
    c = finish(x0[:, 2*LANES:3*LANES] + x0[:, 3*LANES:], x1[:, 2*LANES:3*LANES] + x1[:, 3*LANES:])
    return s, c


def partner(me, k, count):
    if count & (count - 1):
        return lax.rem(me + k, count)
    to = 0
    for i in range(count.bit_length() - 1):
        bit = lax.rem(me // (1 << i), 2)
        to = to + (1 << i) * ((1 - bit) if (k >> i) & 1 else bit)
    return to


def packed_sides(values):
    count = LANES // GHOST
    rows = values.shape[0] // count
    place = lax.broadcasted_iota(jnp.int32, (rows, LANES), 1) // GHOST
    sides = []
    for side in range(2):
        out = None
        for q in range(count):
            piece = values[q * rows : (q + 1) * rows]
            turn = (GHOST * (q - side)) % LANES
            piece = pltpu.roll(piece, turn, 1) if turn else piece
            out = piece if out is None else jnp.where(place == q, piece, out)
        sides.append(out)
    return sides


def unpacked(values, lane_block):
    count = LANES // GHOST
    place = lax.broadcasted_iota(jnp.int32, values.shape, 1) // GHOST
    pieces = []
    for q in range(count):
        turn = (GHOST * (lane_block - q)) % LANES
        piece = pltpu.roll(values, turn, 1) if turn else values
        pieces.append(jnp.where(place == lane_block, piece, 0.0))
    return jnp.concatenate(pieces, axis=0)


def kernel(
    n_dom,
    n_wa,
    fused,
    h_hbm,
    cot_hbm,
    count_hbm,
    src_hbm,
    cos_hbm,
    ws_hbm,
    wt_hbm,
    wm_hbm,
    wf_hbm,
    ga_hbm,
    bond_out,
    *refs,
):
    if fused:
        (g1_out, g2_out, g4_out, g5_out, gg_out) = refs[:5]
        refs = refs[5:]
    else:
        (g_out, gg_out) = refs[:2]
        refs = refs[2:]
    (
        wcat,
        wcat_t,
        h_t,
        gh,
        hot,
        table,
        picked,
        sig_s,
        dcol,
        own_w,
        wbuf,
        wrecv,
        gsend,
        grecv2,
        halo_send,
        halo_recv,
        wsend_sem,
        wrecv_sem,
        nsend_sem,
        nrecv_sem,
        h_ref,
        cot_ref,
        count_ref,
        src_ref,
        cosine_ref,
        ga_ref,
        cos_ref,
        in_sem,
    ) = refs[:28]
    if fused:
        (
            g_full,
            gbuf,
            grecv,
            gsend_sem,
            grecv_sem,
            tbuf,
            trecv,
            tsend_sem,
            trecv_sem,
        ) = refs[28:]
    dom = lax.axis_index("dom")
    wa = lax.axis_index("wa")
    capacity, depth = h_ref.shape
    cols = cot_ref.shape[0]
    up = (lax.rem(dom + 1, n_dom), wa)
    down = (lax.rem(dom + n_dom - 1, n_dom), wa)
    doms = range(1, n_dom) if fused else (1, n_dom - 1)

    barrier = pltpu.get_barrier_semaphore()
    for k in doms:
        pl.semaphore_signal(
            barrier, inc=1, device_id=(lax.rem(dom + k, n_dom), wa), device_id_type=MESH
        )
    for k in range(1, n_wa):
        side = lax.rem(wa + k, n_wa)
        for at in (dom, up[0], down[0]):
            pl.semaphore_signal(barrier, inc=1, device_id=(at, side), device_id_type=MESH)
    loads = []
    pairs = [
        (src_hbm, src_ref),
        (cos_hbm, cosine_ref),
        (h_hbm, h_ref),
        (count_hbm, count_ref),
        (cot_hbm, cot_ref),
        (ga_hbm, ga_ref),
    ]
    for i, w in enumerate((ws_hbm, wm_hbm, wt_hbm, wf_hbm)):
        pairs.append((w, wcat_t.at[pl.ds(i * cols, cols), :]))
    for i, (ours, to) in enumerate(pairs):
        copy = pltpu.make_async_copy(ours, to, in_sem.at[i])
        copy.start()
        loads.append(copy)
    pl.semaphore_wait(barrier, len(doms) + 3 * (n_wa - 1))

    to_up = pltpu.make_async_remote_copy(
        src_ref=h_hbm.at[pl.ds(capacity - GHOST, GHOST), :],
        dst_ref=gh.at[pl.ds(0, GHOST), :],
        send_sem=halo_send.at[0],
        recv_sem=halo_recv.at[0],
        device_id=up,
        device_id_type=MESH,
    )
    to_down = pltpu.make_async_remote_copy(
        src_ref=h_hbm.at[pl.ds(0, GHOST), :],
        dst_ref=gh.at[pl.ds(GHOST, GHOST), :],
        send_sem=halo_send.at[1],
        recv_sem=halo_recv.at[1],
        device_id=down,
        device_id_type=MESH,
    )
    to_up.start()
    to_down.start()

    loads[0].wait()
    loads[1].wait()
    sources, cosines = slot_major(src_ref[...], cosine_ref[...], capacity)
    cos_ref[...] = cosines

    ext = capacity + 2 * GHOST
    row_id = (
        lax.broadcasted_iota(jnp.int32, (capacity, capacity), 0)
        .astype(jnp.float32)
        .astype(jnp.bfloat16)
    )
    one = jnp.ones((), jnp.bfloat16)
    zero = jnp.zeros((), jnp.bfloat16)
    for j in range(ARITY):
        s = sources[15 - j : 16 - j, :]
        after = s >= capacity + GHOST
        own_row = jnp.where((s < GHOST) | after, 512.0, s - GHOST)
        side = jnp.where(s < GHOST, s, jnp.where(after, s - capacity, 512.0))
        here = pl.ds(j * capacity, capacity)
        hot[:capacity, here] = jnp.where(row_id == own_row.astype(jnp.bfloat16), one, zero)
        hot[capacity:, here] = jnp.where(
            row_id[: 2 * GHOST] == side.astype(jnp.bfloat16), one, zero
        )
    for copy in loads[2:]:
        copy.wait()
    h_t[:, :capacity] = flipped(h_ref[...]).astype(jnp.bfloat16)
    wcat[...] = flipped(wcat_t[...]).astype(jnp.bfloat16)
    proj = dot_nt(wcat_t[...], h_ref[...])
    lane = lax.broadcasted_iota(jnp.int32, (1, capacity), 1)
    count = count_ref[0]
    live = jnp.where(
        (lane < count - GHOST) | (lane >= capacity - GHOST), 1.0, 0.0
    ).astype(jnp.float32)
    cot_live = cot_ref[...].astype(jnp.float32) * live
    angle = jnp.broadcast_to(ga_ref[...], (LANES, cols)).T
    high, low = split(proj[: 2 * cols])
    table[: 2 * cols, :capacity] = high
    table[2 * cols :, :capacity] = low

    to_up.wait()
    to_down.wait()
    proj_g = dot_nt(wcat_t[: 2 * cols, :], gh[...])
    high, low = split(proj_g)
    table[: 2 * cols, capacity:] = high
    table[2 * cols :, capacity:] = low
    h_t[:, capacity:] = flipped(gh[...]).astype(jnp.bfloat16)

    picked[...] = dot(table[...], hot[...])

    parts_z = []
    parts_t = []
    gate_sum = jnp.zeros((cols, LANES), jnp.float32)
    for half in range(capacity // LANES):
        at = half * LANES
        q2 = proj[2 * cols : 3 * cols, at : at + LANES]
        base = proj[3 * cols :, at : at + LANES]
        lv = live[:, at : at + LANES]
        numer = jnp.zeros((cols, LANES), jnp.float32)
        denom = jnp.zeros((cols, LANES), jnp.float32)
        for j in range(ARITY):
            here = pl.ds(j * capacity + at, LANES)
            p1 = picked[0:cols, here] + picked[2 * cols : 3 * cols, here]
            p4 = picked[cols : 2 * cols, here] + picked[3 * cols :, here]
            pre = p1 + q2 + cos_ref[15 - j : 16 - j, at : at + LANES] * angle
            sig = jax.nn.sigmoid(pre)
            sig_s[:, here] = sig
            picked[cols : 2 * cols, here] = p4
            numer = numer + sig * p4
            denom = denom + sig
        inverse = 1.0 / (denom * lv + epsilon)
        agg = numer * lv * inverse
        z = base + agg
        sz = jax.nn.sigmoid(z)
        dz = cot_live[:, at : at + LANES] * (sz * (1.0 + z * (1.0 - sz)))
        dnum = dz * inverse
        dq2 = jnp.zeros((cols, LANES), jnp.float32)
        for j in range(ARITY):
            here = pl.ds(j * capacity + at, LANES)
            sig = sig_s[:, here]
            dmsg = sig * dnum
            dpre = dmsg * (picked[cols : 2 * cols, here] - agg) * (1.0 - sig)
            dq2 = dq2 + dpre
            gate_sum = gate_sum + cos_ref[15 - j : 16 - j, at : at + LANES] * dpre
            dcol[:cols, here] = dpre.astype(jnp.bfloat16)
            dcol[cols:, here] = dmsg.astype(jnp.bfloat16)
        parts_z.append(dz.astype(jnp.bfloat16))
        parts_t.append(dq2.astype(jnp.bfloat16))

    high, low = split(gate_sum)
    ones = jnp.ones((16, LANES), jnp.bfloat16)
    gate_row = (dot_nt(ones, high) + dot_nt(ones, low))[0:1]
    gcopies = []
    if fused:
        tbuf[:, :cols] = gate_row
        tbuf[:, cols:] = jnp.zeros((1, LANES - cols), jnp.float32)
        for k in range(1, n_dom):
            copy = pltpu.make_async_remote_copy(
                src_ref=tbuf,
                dst_ref=trecv.at[k - 1],
                send_sem=tsend_sem.at[k - 1],
                recv_sem=trecv_sem.at[k - 1],
                device_id=(lax.rem(dom + k, n_dom), wa),
                device_id_type=MESH,
            )
            copy.start()
            gcopies.append(copy)

    dghost = dot_nt(dcol[...], hot[capacity:, :]).astype(jnp.bfloat16)
    whole_g = dot(wcat[:, : 2 * cols], dghost)
    whole_g = jnp.concatenate(
        [whole_g, jnp.zeros((depth, LANES - 2 * GHOST), jnp.float32)], axis=1
    )
    for c in range(n_wa):
        before, after = packed_sides(whole_g[c * cols : (c + 1) * cols])
        gsend[0, c] = after.astype(jnp.bfloat16)
        gsend[1, c] = before.astype(jnp.bfloat16)
    ncopies = []
    for k in range(n_wa):
        side = lax.rem(wa + k, n_wa)
        for i, to in enumerate((up[0], down[0])):
            copy = pltpu.make_async_remote_copy(
                src_ref=gsend.at[i, side],
                dst_ref=grecv2.at[i, k],
                send_sem=nsend_sem.at[i, k],
                recv_sem=nrecv_sem.at[i, k],
                device_id=(to, side),
                device_id_type=MESH,
            )
            copy.start()
            ncopies.append(copy)

    rows = dot_nt(dcol[...], hot[:capacity, :]).astype(jnp.bfloat16)
    dcat = jnp.concatenate(
        [rows, jnp.concatenate(parts_t, axis=1), jnp.concatenate(parts_z, axis=1)], axis=0
    )
    grads = dot_nt(h_t[:, :capacity], dcat)
    grads_g = dot_nt(h_t[:, capacity:], dghost)
    grads = jnp.concatenate([grads[:, : 2 * cols] + grads_g, grads[:, 2 * cols :]], axis=1)
    if fused:
        chunk = depth // n_dom
        g_full[...] = grads
        for i in range(n_dom):
            gbuf[i] = grads[i * chunk : (i + 1) * chunk].astype(jnp.bfloat16)
        for k in range(n_dom - 1, 0, -1):
            to = partner(dom, k, n_dom)
            copy = pltpu.make_async_remote_copy(
                src_ref=gbuf.at[to],
                dst_ref=grecv.at[k - 1],
                send_sem=gsend_sem.at[k - 1],
                recv_sem=grecv_sem.at[k - 1],
                device_id=(to, wa),
                device_id_type=MESH,
            )
            copy.start()
            gcopies.append(copy)
    else:
        g_out[...] = grads
        gg_out[...] = gate_row

    whole = dot(wcat[...], dcat)
    own_w[...] = whole
    for c in range(n_wa):
        wbuf[c] = whole[c * cols : (c + 1) * cols].astype(jnp.bfloat16)
    wcopies = []
    for k in range(1, n_wa):
        to = lax.rem(wa + k, n_wa)
        copy = pltpu.make_async_remote_copy(
            src_ref=wbuf.at[to],
            dst_ref=wrecv.at[k - 1],
            send_sem=wsend_sem.at[k - 1],
            recv_sem=wrecv_sem.at[k - 1],
            device_id=(dom, to),
            device_id_type=MESH,
        )
        copy.start()
        wcopies.append(copy)

    for copy in wcopies:
        copy.wait()
    mine = pl.ds(pl.multiple_of(wa * cols, cols), cols)
    total = own_w[mine, :]
    for k in range(n_wa - 1):
        total = total + wrecv[k].astype(jnp.float32)
    own = total + cot_live
    if fused:
        for copy in gcopies:
            copy.wait()
        acc = g_full[pl.ds(pl.multiple_of(dom * chunk, chunk), chunk), :]
        gate = gate_row
        for k in range(n_dom - 1):
            acc = acc + grecv[k].astype(jnp.float32)
            gate = gate + trecv[k][:, :cols]
        g1_out[...] = acc[:, :cols]
        g4_out[...] = acc[:, cols : 2 * cols]
        g2_out[...] = acc[:, 2 * cols : 3 * cols]
        g5_out[...] = acc[:, 3 * cols :]
        gg_out[...] = gate

    for copy in ncopies:
        copy.wait()
    below = jnp.zeros(grecv2.shape[2:], jnp.float32)
    above = jnp.zeros(grecv2.shape[2:], jnp.float32)
    for k in range(n_wa):
        below = below + grecv2[0, k].astype(jnp.float32)
        above = above + grecv2[1, k].astype(jnp.float32)
    first = own[:, :LANES] + unpacked(below, 0)
    last = own[:, capacity - LANES :] + unpacked(above, LANES // GHOST - 1)
    result = jnp.concatenate([first, own[:, LANES : capacity - LANES], last], axis=1) if capacity > 2 * LANES else jnp.concatenate([first, last], axis=1)
    bond_out[...] = result.astype(jnp.bfloat16)


def put_out(*refs):
    count = len(refs) // 2
    sem = refs[-1]
    copies = [
        pltpu.make_async_copy(refs[i], refs[count + i], sem.at[i]) for i in range(count)
    ]
    for copy in copies:
        copy.start()
    for copy in copies:
        copy.wait()


def per_device(
    n_dom,
    n_wa,
    bond_feats,
    cotangent,
    bond_count,
    source,
    cosine,
    w_source,
    w_target,
    w_message,
    w_self,
    gate_angle,
):
    capacity, depth = bond_feats.shape
    cols = cotangent.shape[1]
    angles = source.shape[0]
    ext = capacity + 2 * GHOST
    chunk = depth // n_dom
    fused = chunk % 16 == 0
    src = source.reshape(angles // LANES, LANES)
    cos = cosine.reshape(angles // LANES, LANES)
    f32, bf16 = jnp.float32, jnp.bfloat16
    vmem = pl.BlockSpec(memory_space=pltpu.VMEM)
    outs = [jax.ShapeDtypeStruct((cols, capacity), bf16)]
    if fused:
        outs += [jax.ShapeDtypeStruct((chunk, cols), f32)] * 4
    else:
        outs += [jax.ShapeDtypeStruct((depth, 4 * cols), f32)]
    outs += [jax.ShapeDtypeStruct((1, cols), f32)]
    dma = pltpu.SemaphoreType.DMA
    scratch = [
        pltpu.VMEM((depth, 4 * cols), bf16),
        pltpu.VMEM((4 * cols, depth), bf16),
        pltpu.VMEM((depth, ext), bf16),
        pltpu.VMEM((2 * GHOST, depth), bf16),
        pltpu.VMEM((ext, angles), bf16),
        pltpu.VMEM((4 * cols, ext), bf16),
        pltpu.VMEM((4 * cols, angles), f32),
        pltpu.VMEM((cols, angles), f32),
        pltpu.VMEM((2 * cols, angles), bf16),
        pltpu.VMEM((depth, capacity), f32),
        pltpu.VMEM((n_wa, cols, capacity), bf16),
        pltpu.VMEM((n_wa - 1, cols, capacity), bf16),
        pltpu.VMEM((2, n_wa, cols * GHOST // LANES, LANES), bf16),
        pltpu.VMEM((2, n_wa, cols * GHOST // LANES, LANES), bf16),
        dma((2,)),
        dma((2,)),
        dma((n_wa - 1,)),
        dma((n_wa - 1,)),
        dma((2, n_wa)),
        dma((2, n_wa)),
        pltpu.VMEM((capacity, depth), bf16),
        pltpu.VMEM((cols, capacity), bf16),
        pltpu.SMEM((1,), jnp.int32),
        pltpu.VMEM((angles // LANES, LANES), jnp.int32),
        pltpu.VMEM((angles // LANES, LANES), f32),
        pltpu.VMEM((1, cols), f32),
        pltpu.VMEM((16, capacity), f32),
        dma((10,)),
    ]
    if fused:
        scratch += [
            pltpu.VMEM((depth, 4 * cols), f32),
            pltpu.VMEM((n_dom, chunk, 4 * cols), bf16),
            pltpu.VMEM((n_dom - 1, chunk, 4 * cols), bf16),
            dma((n_dom - 1,)),
            dma((n_dom - 1,)),
            pltpu.VMEM((1, LANES), f32),
            pltpu.VMEM((n_dom - 1, 1, LANES), f32),
            dma((n_dom - 1,)),
            dma((n_dom - 1,)),
        ]
    results = pl.pallas_call(
        functools.partial(kernel, n_dom, n_wa, fused),
        out_shape=outs,
        in_specs=[pl.BlockSpec(memory_space=pltpu.HBM)] * 10,
        out_specs=[vmem] * len(outs),
        scratch_shapes=scratch,
        compiler_params=pltpu.CompilerParams(
            collective_id=0, has_side_effects=True, vmem_limit_bytes=48 << 20
        ),
        name="line_graph_backward",
    )(
        *(
            operand
            if operand.size == 1
            else pltpu.with_memory_space_constraint(operand, pltpu.HBM)
            for operand in (
                bond_feats,
                cotangent.T,
                bond_count,
                src,
                cos,
                w_source.T,
                w_target.T,
                w_message.T,
                w_self.T,
                gate_angle.reshape(1, cols),
            )
        )
    )
    if fused:
        bond_grad, one, two, four, five, gate = pl.pallas_call(
            put_out,
            out_shape=outs,
            in_specs=[vmem] * len(outs),
            out_specs=[pl.BlockSpec(memory_space=pltpu.HBM)] * len(outs),
            scratch_shapes=[dma((len(outs),))],
            name="put_out",
        )(*(pltpu.with_memory_space_constraint(r, pltpu.VMEM) for r in results))
        return bond_grad.T, one, two, four, five, gate.reshape(cols)
    bond_grad, grads, gate = results
    mine = lax.psum_scatter(grads, "dom", scatter_dimension=0, tiled=True)
    gate = lax.psum(gate.reshape(cols), "dom")
    one, four, two, five = (mine[:, i * cols : (i + 1) * cols] for i in range(4))
    return bond_grad.T, one, two, four, five, gate


def solution(mesh):
    return jax.shard_map(
        functools.partial(per_device, mesh.shape["dom"], mesh.shape["wa"]),
        mesh=mesh,
        in_specs=(
            P("dom", None),
            P("dom", "wa"),
            P("dom"),
            P("dom"),
            P("dom"),
            P(None, "wa"),
            P(None, "wa"),
            P(None, "wa"),
            P(None, "wa"),
            P("wa"),
        ),
        out_specs=(
            P("dom", "wa"),
            P("dom", "wa"),
            P("dom", "wa"),
            P("dom", "wa"),
            P("dom", "wa"),
            P("wa"),
        ),
        check_vma=False,
    )
```
